256 devices in a mesh: ep: 32 (over z, y), tp: 8 (over x, core).
Axes of the slice: x: 4, y: 4, z: 8, core: 2. Of those that a mesh axis runs over, the one named last changes fastest.
Arguments:
- tokens: bfloat16 [4096, 2048], P('ep', 'tp'), may hold values from -200 to 200
- norm_gain: bfloat16 [2048], P('tp'), may hold values from 0.099609375 to 1.8984375
- router_logits: float32 [4096, 64], P('ep'), may hold values from -8 to 400
- routes: int32 [4096, 8], P('ep'), may hold values from 0 to 63, all different within a row; in each aligned block of 128 rows (0 to 127, 128 to 255, ...) at most 32 rows name the same one
- gate_proj: bfloat16 [64, 2048, 1024], P('ep', None, 'tp'), may hold values from -0.125 to 0.125
- up_proj: bfloat16 [64, 2048, 1024], P('ep', None, 'tp'), may hold values from -0.125 to 0.125
- down_proj: bfloat16 [64, 1024, 2048], P('ep', 'tp'), may hold values from -0.1875 to 0.1875
Outputs:
- mixed: bfloat16 [4096, 2048], P('ep', 'tp')
The draws below stay inside these ranges and needn't reach their ends.
Inputs may be any that keep to these rules, and one draw needn't show every extreme that they name: `routes`: within each aligned block of 128 rows (the tokens of one index of ep) no expert is named by more than 32 rows, a bound that some block reaches; a row names 8 different experts.
All inputs are finite; a program needn't handle non-finite values.
Results may differ from the reference program's by a relative error of at most 0.0071.
Values may be sent and summed in bfloat16 or wider, within the bound.
No kernel may reach another device: no remote copies, remote signals or barrier semaphores. Data moves between devices by JAX's collectives and lax.ppermute only.
A program may use at most 128 MiB of HBM per device.

```python
import math
import jax
import jax.numpy as jnp
import numpy as np
from jax import lax

D = 2048
FF = 1024
TOP = 8
TOK_GRP = 128
EXPERTS = 64
CAP = 32
TOKENS = 4096
N_EP = 32


def draw_tokens(key, part):
    key_col, key_row, key_noise = jax.random.split(key, 3)
    columns = jnp.arange(D, dtype=jnp.float32) / D
    col_scale = 10.0 ** (0.5 * columns + 0.5 * jax.random.uniform(key_col, (D,), jnp.float32))
    row_scale = 0.3 * 10.0 ** jax.random.uniform(key_row, (TOKENS, 1), jnp.float32)
    noise = jnp.clip(jax.random.normal(key_noise, (TOKENS, D), jnp.float32), -6.0, 6.0)
    return (noise * row_scale * col_scale[None, :]).astype(jnp.bfloat16)


def draw_router_logits(key, part):
    key_base = jax.random.fold_in(key, 0)
    values = jnp.clip(0.5 * jax.random.normal(key_base, (TOKENS, EXPERTS), jnp.float32), -8.0, 8.0)
    return values.astype(jnp.float32)


def level_of(own_key, dims, cuts, least, top_value):
    loudness, own = 1.0, jax.random.fold_in(own_key, 6)
    for axis_at, shards_of in cuts:
        heights = jnp.exp(jax.random.uniform(jax.random.fold_in(own, axis_at), (shards_of,), jnp.float32, least / len(cuts), top_value / len(cuts)))
        loudness = loudness * jnp.repeat(heights, dims[axis_at] // shards_of).reshape([-1 if axis == axis_at else 1 for axis in range(len(dims))])
    return loudness


def shared_out(stream_key, own, number, rows, number_of, top, reach, lean):
    order = jax.random.permutation(stream_key, number_of)
    heavy_load, usual = load_shares(number_of, rows * top, reach, lean, True), load_shares(number_of, rows * top, reach, lean, False)
    places = jnp.arange(number_of)

    def named(tallies, offset_by):
        used = int((tallies > 0).sum())
        fixed = max(1, used // 4)
        moved = fixed + (places - fixed + offset_by * (used - fixed)) % max(1, number_of - fixed)
        return jnp.zeros((number_of,), jnp.int32).at[order[jnp.where(places < fixed, places, moved)]].set(jnp.asarray(tallies, jnp.int32))

    tallies = jnp.where(number % 4 == 0, named(heavy_load, number // 4), named(usual, number - number // 4 - 1))
    mixed = jax.random.permutation(jax.random.fold_in(own, 3), number_of)
    donor, sink = mixed[0:number_of // 2 * 2:2], mixed[1:number_of // 2 * 2:2]
    margin = jnp.minimum(tallies[donor] - 1, reach - tallies[sink]) // 2
    margin = jnp.where((donor == order[0]) | (sink == order[0]) | (tallies[sink] == 0), 0, jnp.maximum(margin, 0))
    moved = jax.random.randint(jax.random.fold_in(own, 4), (number_of // 2,), 0, 1 << 20) % (margin + 1)
    tallies = tallies.at[donor].add(-moved).at[sink].add(moved)
    items = jnp.searchsorted(jnp.cumsum(tallies), jnp.arange(rows * top), side="right").astype(jnp.int32)
    grid = items.reshape(top, rows).T
    grid = grid[jax.random.permutation(jax.random.fold_in(own, 1), rows)]
    offset_by = jax.random.randint(jax.random.fold_in(own, 2), (rows, 1), 0, top)
    return jnp.take_along_axis(grid, (jnp.arange(top)[None, :] + offset_by) % top, axis=1)


def load_shares(count, total, limit, slope, full):
    portions = [(1 << 20) // math.isqrt(standing ** slope) + 1 for standing in range(1, count + 1)]
    largest = limit if full else min(limit, max(-(-total // count), total * portions[0] // sum(portions)))
    least = 1 if total - largest >= count - 1 else 0
    holding, surplus = [largest] + [least] * (count - 1), total - largest - least * (count - 1)
    while surplus > 0:
        free = [i for i in range(1, count) if holding[i] < largest] or [i for i in range(1, count) if holding[i] < limit]
        pool, budget = sum([portions[i] for i in free]), surplus
        for i in free:
            more = min(limit - holding[i], max(1, budget * portions[i] // pool), surplus)
            holding[i] = holding[i] + more
            surplus = surplus - more
    return np.array(holding)


def bell_draw(rng, extent, deviation, most, pieces=(), kind=jnp.bfloat16):
    drawn = jax.random.normal(rng, extent, jnp.float32) * deviation
    if len(pieces) > 0:
        drawn = level_of(rng, extent, pieces, -0.22, 0.18) * drawn
    return jnp.clip(drawn, min=-most, max=most).astype(kind)


def setup_inputs(seed: int = 0) -> dict:
    keys = jax.random.split(jax.random.key(seed), 8)
    tokens = draw_tokens(jax.random.fold_in(keys[7], 71), 0)
    norm_gain = jnp.clip(1.0 + 0.18 * jax.random.normal(keys[1], (D,), jnp.float32), 0.099609375, 1.8984375).astype(jnp.bfloat16)
    router_logits = draw_router_logits(jax.random.fold_in(keys[7], 71), 0)
    routes_keys = jax.random.split(jax.random.fold_in(keys[3], 1), TOKENS // TOK_GRP)
    routes_turns = jax.random.permutation(jax.random.fold_in(keys[3], 3), TOKENS // TOK_GRP)
    routes = jax.vmap(lambda own, number: shared_out(jax.random.fold_in(keys[3], 2), own, number, TOK_GRP, EXPERTS, TOP, CAP, 2))(routes_keys, routes_turns).reshape((TOKENS, TOP))
    gate_proj = bell_draw(keys[4], (EXPERTS, D, FF), D ** -0.5, 0.125, ((0, 32), (2, 8)))
    up_proj = bell_draw(keys[5], (EXPERTS, D, FF), D ** -0.5, 0.125, ((0, 32), (2, 8)))
    down_proj = bell_draw(keys[6], (EXPERTS, FF, D), FF ** -0.5, 0.1875, ((0, 32), (1, 8)))
    return dict(tokens=tokens, norm_gain=norm_gain, router_logits=router_logits, routes=routes, gate_proj=gate_proj, up_proj=up_proj, down_proj=down_proj)


epsilon = 1e-05

def reference(tokens, norm_gain, router_logits, routes, gate_proj, up_proj, down_proj):
    floated = tokens.astype(jnp.float32)
    mean_square = lax.optimization_barrier(jnp.mean(floated * floated, axis=-1, keepdims=True))
    normed = (floated * lax.rsqrt(mean_square + epsilon) * norm_gain.astype(jnp.float32)).astype(jnp.bfloat16)
    chosen = jnp.take_along_axis(router_logits, routes, axis=1)
    gates = jax.nn.softmax(chosen, axis=-1)
    grouped = routes.reshape(N_EP, TOK_GRP * TOP).astype(jnp.int32)
    hits = (grouped[:, :, None] == jnp.arange(EXPERTS, dtype=jnp.int32)[None, None, :]).astype(jnp.int32)
    position = lax.optimization_barrier(jnp.sum((jnp.cumsum(hits, axis=1) - hits) * hits, axis=-1)).astype(jnp.int32)
    source = jnp.arange(N_EP, dtype=jnp.int32)[:, None]
    flat_index = (grouped * (N_EP * CAP) + source * CAP + position).reshape(-1).astype(jnp.int32)
    token_index = (jnp.arange(TOKENS * TOP, dtype=jnp.int32) // TOP).astype(jnp.int32)
    buffer_tok = jnp.full((EXPERTS * N_EP * CAP,), TOKENS, dtype=jnp.int32).at[flat_index].set(token_index)
    padded = jnp.concatenate([normed, jnp.zeros((1, D), jnp.bfloat16)], axis=0)

    def expert_rows(operands):
        index, w_gate, w_up, w_down = operands
        rows = padded[index]
        gate_val = jnp.dot(rows, w_gate, preferred_element_type=jnp.float32)
        up_val = jnp.dot(rows, w_up, preferred_element_type=jnp.float32)
        hidden = (jax.nn.silu(gate_val) * up_val).astype(jnp.bfloat16)
        return jnp.dot(hidden, w_down, preferred_element_type=jnp.float32).astype(jnp.bfloat16)
    outputs = lax.map(expert_rows, (buffer_tok.reshape(EXPERTS, N_EP * CAP), gate_proj, up_proj, down_proj))
    picked = outputs.reshape(EXPERTS * N_EP * CAP, D)[flat_index].astype(jnp.float32).reshape(TOKENS, TOP, D)
    mixed = jnp.einsum('tk,tkd->td', gates, picked, precision=lax.Precision.HIGHEST)
    return mixed.astype(jnp.bfloat16)
```

```python
import jax
import jax.numpy as jnp
from jax import lax
from jax.sharding import Mesh, PartitionSpec as P

epsilon = 1e-05
chip_cores = 2


def on_device(tokens, norm_gain, router_logits, routes, gate_proj, up_proj, down_proj):
    bf16, f32 = jnp.bfloat16, jnp.float32
    ep_count = lax.axis_size("ep")
    row_count = lax.axis_size("x")
    group_size, width = tokens.shape
    top_count = routes.shape[1]
    expert_count = gate_proj.shape[0] * ep_count
    capacity = 2 * group_size * top_count // expert_count
    core = lax.axis_index("core")
    row = lax.axis_index("x")

    def swap(own):
        keep = lax.dynamic_index_in_dim(own, core, 0, keepdims=False)
        give = lax.dynamic_index_in_dim(own, 1 - core, 0, keepdims=False)
        return keep, lax.ppermute(give, "core", [(0, 1), (1, 0)])

    gate_w = jnp.concatenate(swap(gate_proj), axis=1)
    up_w = jnp.concatenate(swap(up_proj), axis=1)
    down_w = jnp.concatenate(swap(down_proj), axis=0)

    expert_iota = jnp.arange(expert_count, dtype=jnp.int32)
    hits = jnp.any(routes[:, :, None] == expert_iota[None, None, :], axis=1)
    earlier = jnp.tril(jnp.ones((group_size, group_size), bf16), -1)
    position = jnp.dot(earlier, hits.astype(bf16), preferred_element_type=f32)
    shifted = jnp.where(hits, router_logits, -jnp.inf)
    shifted = jnp.exp(shifted - jnp.max(shifted, axis=1, keepdims=True))
    gates = shifted / jnp.sum(shifted, axis=1, keepdims=True)

    def of_core(table):
        return lax.dynamic_index_in_dim(
            table.reshape(group_size, ep_count, chip_cores), core, 2, keepdims=False
        )

    slot = jnp.where(of_core(hits), of_core(position), -1.0)
    gates = of_core(gates)
    slot_iota = jnp.arange(capacity, dtype=jnp.int32).astype(f32)

    stacked = jnp.concatenate([tokens, jnp.broadcast_to(norm_gain[None, :], (16, width))], axis=0)
    whole = lax.all_gather(stacked, ("x", "core"), axis=0, tiled=False)
    floated = whole[:, :group_size].astype(f32)
    mean_square = jnp.sum(floated * floated, axis=(0, 2)) / (width * whole.shape[0])
    mine = lax.dynamic_slice_in_dim(whole, row * chip_cores, chip_cores, 0)
    normed = (
        mine[:, :group_size].astype(f32)
        * lax.rsqrt(mean_square + epsilon)[None, :, None]
        * mine[:, group_size : group_size + 1].astype(f32)
    ).astype(bf16)
    normed = jnp.concatenate([normed[0], normed[1]], axis=1)

    table = (slot.T[:, None, :] == slot_iota[None, :, None]).astype(bf16)
    outgoing = jnp.dot(
        table.reshape(ep_count * capacity, group_size), normed, preferred_element_type=f32
    ).astype(bf16)
    arrived = lax.all_to_all(
        outgoing.reshape(ep_count, capacity, -1), "ep", split_axis=0, concat_axis=0, tiled=True
    ).reshape(ep_count * capacity, -1)
    rows = lax.all_gather(arrived, "x", axis=0, tiled=False)
    part = rows.shape[2]
    gate_val = jnp.einsum(
        "frd,fdh->rh", rows, gate_w.reshape(row_count, part, -1), preferred_element_type=f32
    )
    up_val = jnp.einsum(
        "frd,fdh->rh", rows, up_w.reshape(row_count, part, -1), preferred_element_type=f32
    )
    hidden = (jax.nn.silu(gate_val) * up_val).astype(bf16)
    term = jnp.einsum(
        "rh,hfd->frd", hidden, down_w.reshape(-1, row_count, part), preferred_element_type=f32
    ).astype(bf16)
    summed = lax.psum_scatter(term, "x", scatter_dimension=0, tiled=False)
    returned = lax.all_to_all(
        summed.reshape(ep_count, capacity, -1), "ep", split_axis=0, concat_axis=0, tiled=True
    ).reshape(ep_count * capacity, -1)

    weight = jnp.where(slot[:, :, None] == slot_iota[None, None, :], gates[:, :, None], 0.0)
    weight = weight.reshape(group_size, ep_count * capacity)
    high = lax.reduce_precision(weight, 8, 7)
    both = jnp.concatenate([high.astype(bf16), (weight - high).astype(bf16)], axis=0)
    mixed = jnp.dot(both, returned, preferred_element_type=f32)
    mixed = mixed[:group_size] + mixed[group_size:]
    keep = lax.dynamic_slice_in_dim(mixed, core * width, width, 1)
    give = lax.dynamic_slice_in_dim(mixed, (1 - core) * width, width, 1)
    return (keep + lax.ppermute(give, "core", [(0, 1), (1, 0)])).astype(bf16)


def solution(mesh):
    ep_count, tp_count = mesh.devices.shape
    fine = Mesh(
        mesh.devices.reshape(ep_count, tp_count // chip_cores, chip_cores), ("ep", "x", "core")
    )
    tp = ("x", "core")
    return jax.shard_map(
        on_device,
        mesh=fine,
        in_specs=(
            P("ep", tp),
            P(tp),
            P("ep", None),
            P("ep", None),
            P("ep", None, tp),
            P("ep", None, tp),
            P("ep", tp, None),
        ),
        out_specs=P("ep", tp),
        check_vma=False,
    )
```

```python
import jax
import jax.numpy as jnp
from jax import lax
from jax.experimental import pallas as pl
from jax.experimental.pallas import tpu as pltpu
from jax.sharding import Mesh, PartitionSpec as P

epsilon = 1e-05
chip_cores = 2
other_core = [(0, 1), (1, 0)]
near_chip = [(0, 1), (1, 0), (2, 3), (3, 2)]
cross_chip = [(0, 3), (3, 0), (1, 2), (2, 1)]


def ffn_kernel(core_ref, arrived, across, *refs):
    joined, downs, (keep, give, hidden) = refs[:4], refs[4:8], refs[8:]
    core = core_ref[0]
    f32 = jnp.float32
    rows, held = arrived.shape
    block = 256
    unit = downs[0].shape[0]

    def at(j, parity):
        return pl.ds(pl.multiple_of((2 * j + parity) * block, block), block)

    for k in range(4):
        both = jnp.zeros((rows, 2 * unit), f32)
        for j in range(held // block):
            lanes = pl.ds(j * block, block)
            both += jnp.dot(arrived[:, lanes], joined[k][at(j, core), :], preferred_element_type=f32)
            both += jnp.dot(
                across[:, lanes], joined[k][at(j, 1 - core), :], preferred_element_type=f32
            )
        gate_val, up_val = both[:, :unit], both[:, unit:]
        silu = gate_val / (1.0 + jnp.exp(-gate_val))
        hidden[:, pl.ds(k * unit, unit)] = (silu * up_val).astype(hidden.dtype)
    for parity, out in ((core, keep), (1 - core, give)):
        for j in range(held // block):
            total = jnp.zeros((rows, block), f32)
            for k in range(4):
                total += jnp.dot(
                    hidden[:, pl.ds(k * unit, unit)],
                    downs[k][:, at(j, parity)],
                    preferred_element_type=f32,
                )
            out[:, pl.ds(j * block, block)] = total.astype(out.dtype)


def expert_rows(core, arrived, across, shards):
    rows, held = arrived.shape
    unit, width = shards[0][1].shape
    whole = pl.BlockSpec(memory_space=pltpu.VMEM)
    return pl.pallas_call(
        ffn_kernel,
        out_shape=(
            jax.ShapeDtypeStruct((rows, held), jnp.float32),
            jax.ShapeDtypeStruct((rows, held), jnp.bfloat16),
        ),
        in_specs=[pl.BlockSpec(memory_space=pltpu.SMEM)] + [whole] * 10,
        out_specs=(whole, whole),
        scratch_shapes=[pltpu.VMEM((rows, 4 * unit), jnp.bfloat16)],
        compiler_params=pltpu.CompilerParams(vmem_limit_bytes=40 * 2**20),
        cost_estimate=pl.CostEstimate(
            flops=2 * rows * width * 4 * unit * 3, bytes_accessed=12 * 2**20, transcendentals=0
        ),
    )(
        core.reshape(1).astype(jnp.int32),
        arrived,
        across,
        *[one[0] for one in shards],
        *[one[1] for one in shards],
    )


def on_device(tokens, norm_gain, router_logits, routes, gate_proj, up_proj, down_proj):
    bf16, f32 = jnp.bfloat16, jnp.float32
    ep_count = lax.axis_size("ep")
    row_count = lax.axis_size("x")
    group_size, width = tokens.shape
    local_experts = gate_proj.shape[0]
    top_count = routes.shape[1]
    expert_count = local_experts * ep_count
    capacity = 2 * group_size * top_count // expert_count
    share = capacity // (row_count // local_experts)
    core = lax.axis_index("core")
    row = lax.axis_index("x")
    kind = row // local_experts
    half = row % local_experts

    def pick(at):
        joined = jnp.concatenate([gate_proj, up_proj], axis=2)
        return (
            lax.dynamic_index_in_dim(joined, at, 0, keepdims=False),
            lax.dynamic_index_in_dim(down_proj, at, 0, keepdims=False),
        )

    def send(arrays, pairs):
        return tuple(lax.ppermute(one, "x", pairs) for one in arrays)

    own = pick(kind)
    crossed = send(pick(1 - kind), cross_chip)
    near = send(own, near_chip)
    relayed = send(crossed, near_chip)
    shards = (own, near, crossed, relayed)

    expert_iota = jnp.arange(expert_count, dtype=jnp.int32)
    hits = jnp.any(routes[:, :, None] == expert_iota[None, None, :], axis=1)
    earlier = jnp.tril(jnp.ones((group_size, group_size), bf16), -1)
    position = jnp.dot(earlier, hits.astype(bf16), preferred_element_type=f32)
    shifted = jnp.where(hits, router_logits, -jnp.inf)
    shifted = jnp.exp(shifted - jnp.max(shifted, axis=1, keepdims=True))
    gates = shifted / jnp.sum(shifted, axis=1, keepdims=True)

    def of_kind(table):
        return lax.dynamic_index_in_dim(
            table.reshape(group_size, ep_count, local_experts), kind, 2, keepdims=False
        )

    slot = jnp.where(of_kind(hits), of_kind(position), -1.0)
    gates = of_kind(gates)
    slot_iota = (jnp.arange(share, dtype=jnp.int32) + half * share).astype(f32)

    stacked = jnp.concatenate([tokens, jnp.broadcast_to(norm_gain[None, :], (16, width))], axis=0)
    whole = lax.all_gather(stacked, ("x", "core"), axis=0, tiled=False)
    floated = whole[:, :group_size].astype(f32)
    mean_square = jnp.sum(floated * floated, axis=(0, 2)) / (width * whole.shape[0])
    mine = lax.dynamic_index_in_dim(
        whole.reshape(row_count, chip_cores, -1, width), core, 1, keepdims=False
    )
    normed = (
        mine[:, :group_size].astype(f32)
        * lax.rsqrt(mean_square + epsilon)[None, :, None]
        * mine[:, group_size : group_size + 1].astype(f32)
    ).astype(bf16)
    normed = jnp.concatenate([normed[j] for j in range(row_count)], axis=1)

    table = (slot.T[:, None, :] == slot_iota[None, :, None]).astype(bf16)
    outgoing = jnp.dot(
        table.reshape(ep_count * share, group_size), normed, preferred_element_type=f32
    ).astype(bf16)
    arrived = lax.all_to_all(
        outgoing.reshape(ep_count, share, -1), "ep", split_axis=0, concat_axis=0, tiled=True
    ).reshape(ep_count * share, -1)
    across = lax.ppermute(arrived, "core", other_core)
    keep, give = expert_rows(core, arrived, across, shards)
    summed = keep + lax.ppermute(give, "core", other_core).astype(f32)
    returned = lax.all_to_all(
        summed.astype(bf16).reshape(ep_count, share, -1), "ep", split_axis=0, concat_axis=0, tiled=True
    ).reshape(ep_count * share, -1)

    weight = jnp.where(slot[:, :, None] == slot_iota[None, None, :], gates[:, :, None], 0.0)
    weight = weight.reshape(group_size, ep_count * share)
    high = lax.reduce_precision(weight, 8, 7)
    both = jnp.concatenate([high.astype(bf16), (weight - high).astype(bf16)], axis=0)
    mixed = jnp.dot(both, returned, preferred_element_type=f32)
    mixed = mixed[:group_size] + mixed[group_size:]

    def block_of(step):
        return lax.dynamic_slice_in_dim(mixed, ((row + step) % row_count) * width, width, 1)

    result = block_of(0)
    for step in range(1, row_count):
        pairs = [(at, (at + step) % row_count) for at in range(row_count)]
        result = result + lax.ppermute(block_of(step), "x", pairs)
    return result.astype(bf16)


def solution(mesh):
    ep_count, tp_count = mesh.devices.shape
    fine = Mesh(
        mesh.devices.reshape(ep_count, tp_count // chip_cores, chip_cores), ("ep", "x", "core")
    )
    tp = ("x", "core")
    return jax.shard_map(
        on_device,
        mesh=fine,
        in_specs=(
            P("ep", tp),
            P(tp),
            P("ep", None),
            P("ep", None),
            P("ep", None, tp),
            P("ep", None, tp),
            P("ep", tp, None),
        ),
        out_specs=P("ep", tp),
        check_vma=False,
    )
```

```python
import functools
import jax
import jax.numpy as jnp
from jax import lax
from jax.experimental import pallas as pl
from jax.experimental.pallas import tpu as pltpu
from jax.sharding import Mesh, PartitionSpec as P

epsilon = 1e-05
chip_cores = 2
block = 256
other_core = [(0, 1), (1, 0)]
near_chip = [(0, 1), (1, 0), (2, 3), (3, 2)]
cross_chip = [(0, 3), (3, 0), (1, 2), (2, 1)]


def pick_kernel(kind_ref, gate, up, down, own, other, sems):
    depth, unit = gate.shape[1:]
    copies = []
    for turn, packed in enumerate((own, other)):
        at = kind_ref[0] if turn == 0 else 1 - kind_ref[0]
        pairs = [
            (gate.at[at], packed.at[pl.ds(0, depth), pl.ds(0, unit)]),
            (up.at[at], packed.at[pl.ds(0, depth), pl.ds(unit, unit)]),
        ]
        for j in range(depth // block):
            rows = pl.ds(depth + j * unit, unit)
            pairs.append((down.at[at, :, pl.ds(j * block, block)], packed.at[rows, :]))
        for source, target in pairs:
            copies.append(pltpu.make_async_copy(source, target, sems.at[len(copies)]))
    for copy in copies:
        copy.start()
    for copy in copies:
        copy.wait()


def pick_shards(kind, gate, up, down):
    anywhere = pl.BlockSpec(memory_space=pl.ANY)
    depth, unit = gate.shape[1:]
    packed = jax.ShapeDtypeStruct((depth + depth // block * unit, block), gate.dtype)
    return pl.pallas_call(
        pick_kernel,
        out_shape=(packed, packed),
        in_specs=[pl.BlockSpec(memory_space=pltpu.SMEM)] + [anywhere] * 3,
        out_specs=(anywhere,) * 2,
        scratch_shapes=[pltpu.SemaphoreType.DMA((2 * (2 + depth // block),))],
        cost_estimate=pl.CostEstimate(flops=0, bytes_accessed=12 * 2**20, transcendentals=0),
    )(kind.reshape(1).astype(jnp.int32), gate, up, down)


def ffn_kernel(count, core_ref, arrived, across, *refs):
    shards, added, (keep, give, hidden) = refs[:count], refs[count:-3], refs[-3:]
    core = core_ref[0]
    f32 = jnp.float32
    rows, held = arrived.shape
    depth = 2 * held
    unit = block // 2

    def at(j, parity):
        return pl.ds(pl.multiple_of((2 * j + parity) * block, block), block)

    def down_at(j, parity):
        return pl.ds(pl.multiple_of(depth + (2 * j + parity) * unit, unit), unit)

    for k, shard in enumerate(shards):
        both = jnp.zeros((rows, block), f32)
        for j in range(held // block):
            lanes = pl.ds(j * block, block)
            both += jnp.dot(arrived[:, lanes], shard[at(j, core), :], preferred_element_type=f32)
            both += jnp.dot(across[:, lanes], shard[at(j, 1 - core), :], preferred_element_type=f32)
        gate_val, up_val = both[:, :unit], both[:, unit:]
        silu = gate_val / (1.0 + jnp.exp(-gate_val))
        hidden[:, pl.ds(k * unit, unit)] = (silu * up_val).astype(hidden.dtype)
    for which, (parity, out) in enumerate(((core, keep), (1 - core, give))):
        for j in range(held // block):
            lanes = pl.ds(j * block, block)
            total = added[which][:, lanes] if added else jnp.zeros((rows, block), f32)
            for k, shard in enumerate(shards):
                total += jnp.dot(
                    hidden[:, pl.ds(k * unit, unit)],
                    shard[down_at(j, parity), :],
                    preferred_element_type=f32,
                )
            out[:, lanes] = total.astype(out.dtype)


def expert_rows(core, arrived, across, shards, added, give_type):
    rows, held = arrived.shape
    unit, width, count = block // 2, 2 * held, len(shards)
    whole = pl.BlockSpec(memory_space=pltpu.VMEM)
    return pl.pallas_call(
        functools.partial(ffn_kernel, count),
        out_shape=(
            jax.ShapeDtypeStruct((rows, held), jnp.float32),
            jax.ShapeDtypeStruct((rows, held), give_type),
        ),
        in_specs=[pl.BlockSpec(memory_space=pltpu.SMEM)] + [whole] * (2 + count + len(added)),
        out_specs=(whole, whole),
        scratch_shapes=[pltpu.VMEM((rows, count * unit), jnp.bfloat16)],
        compiler_params=pltpu.CompilerParams(vmem_limit_bytes=40 * 2**20),
        cost_estimate=pl.CostEstimate(
            flops=2 * rows * width * unit, bytes_accessed=2**20, transcendentals=0
        ),
    )(core.reshape(1).astype(jnp.int32), arrived, across, *shards, *added)


def on_device(tokens, norm_gain, router_logits, routes, gate_proj, up_proj, down_proj):
    bf16, f32 = jnp.bfloat16, jnp.float32
    ep_count = lax.axis_size("ep")
    row_count = lax.axis_size("x")
    group_size, width = tokens.shape
    local_experts = gate_proj.shape[0]
    top_count = routes.shape[1]
    expert_count = local_experts * ep_count
    capacity = 2 * group_size * top_count // expert_count
    share = capacity // (row_count // local_experts)
    core = lax.axis_index("core")
    row = lax.axis_index("x")
    kind = row // local_experts
    half = row % local_experts

    own, other = pick_shards(kind, gate_proj, up_proj, down_proj)
    tokens, own, other = lax.optimization_barrier((tokens, own, other))

    crossed = lax.ppermute(other, "x", cross_chip)
    near = lax.ppermute(own, "x", near_chip)
    crossed, near = lax.optimization_barrier((crossed, near))
    relayed = lax.ppermute(crossed, "x", near_chip)

    expert_iota = jnp.arange(expert_count, dtype=jnp.int32)
    hits = jnp.any(routes[:, :, None] == expert_iota[None, None, :], axis=1)
    earlier = jnp.tril(jnp.ones((group_size, group_size), bf16), -1)
    position = jnp.dot(earlier, hits.astype(bf16), preferred_element_type=f32)
    shifted = jnp.where(hits, router_logits, -jnp.inf)
    shifted = jnp.exp(shifted - jnp.max(shifted, axis=1, keepdims=True))
    gates = shifted / jnp.sum(shifted, axis=1, keepdims=True)

    def of_kind(table):
        return lax.dynamic_index_in_dim(
            table.reshape(group_size, ep_count, local_experts), kind, 2, keepdims=False
        )

    slot = jnp.where(of_kind(hits), of_kind(position), -1.0)
    gates = of_kind(gates)
    slot_iota = (jnp.arange(share, dtype=jnp.int32) + half * share).astype(f32)

    stacked = jnp.concatenate([tokens, jnp.broadcast_to(norm_gain[None, :], (16, width))], axis=0)
    whole = lax.all_gather(stacked, ("x", "core"), axis=0, tiled=False)
    floated = whole[:, :group_size].astype(f32)
    mean_square = jnp.sum(floated * floated, axis=(0, 2)) / (width * whole.shape[0])
    mine = lax.dynamic_index_in_dim(
        whole.reshape(row_count, chip_cores, -1, width), core, 1, keepdims=False
    )
    normed = (
        mine[:, :group_size].astype(f32)
        * lax.rsqrt(mean_square + epsilon)[None, :, None]
        * mine[:, group_size : group_size + 1].astype(f32)
    ).astype(bf16)
    normed = jnp.concatenate([normed[j] for j in range(row_count)], axis=1)

    table = (slot.T[:, None, :] == slot_iota[None, :, None]).astype(bf16)
    outgoing = jnp.dot(
        table.reshape(ep_count * share, group_size), normed, preferred_element_type=f32
    ).astype(bf16)
    arrived = lax.all_to_all(
        outgoing.reshape(ep_count, share, -1), "ep", split_axis=0, concat_axis=0, tiled=True
    ).reshape(ep_count * share, -1)
    across = lax.ppermute(arrived, "core", other_core)
    added = expert_rows(core, arrived, across, (own, near, crossed), (), f32)
    keep, give = expert_rows(core, arrived, across, (relayed,), added, bf16)
    summed = keep + lax.ppermute(give, "core", other_core).astype(f32)
    returned = lax.all_to_all(
        summed.astype(bf16).reshape(ep_count, share, -1), "ep", split_axis=0, concat_axis=0, tiled=True
    ).reshape(ep_count * share, -1)

    weight = jnp.where(slot[:, :, None] == slot_iota[None, None, :], gates[:, :, None], 0.0)
    weight = weight.reshape(group_size, ep_count * share)
    high = lax.reduce_precision(weight, 8, 7)
    both = jnp.concatenate([high.astype(bf16), (weight - high).astype(bf16)], axis=0)
    mixed = jnp.dot(both, returned, preferred_element_type=f32)
    mixed = mixed[:group_size] + mixed[group_size:]

    def block_of(step):
        return lax.dynamic_slice_in_dim(mixed, ((row + step) % row_count) * width, width, 1)

    result = block_of(0)
    for step in range(1, row_count):
        pairs = [(at, (at + step) % row_count) for at in range(row_count)]
        result = result + lax.ppermute(block_of(step), "x", pairs)
    return result.astype(bf16)


def solution(mesh):
    ep_count, tp_count = mesh.devices.shape
    fine = Mesh(
        mesh.devices.reshape(ep_count, tp_count // chip_cores, chip_cores), ("ep", "x", "core")
    )
    tp = ("x", "core")
    return jax.shard_map(
        on_device,
        mesh=fine,
        in_specs=(
            P("ep", tp),
            P(tp),
            P("ep", None),
            P("ep", None),
            P("ep", None, tp),
            P("ep", None, tp),
            P("ep", tp, None),
        ),
        out_specs=P("ep", tp),
        check_vma=False,
    )
```

```python
import functools
import jax
import jax.numpy as jnp
from jax import lax
from jax.experimental import pallas as pl
from jax.experimental.pallas import tpu as pltpu
from jax.sharding import Mesh, PartitionSpec as P

epsilon = 1e-05
chip_cores = 2
block = 256
other_core = [(0, 1), (1, 0)]
near_chip = [(0, 1), (1, 0), (2, 3), (3, 2)]
cross_chip = [(0, 3), (3, 0), (1, 2), (2, 1)]


def pick_kernel(kind_ref, *refs):
    unit = refs[0].shape[2]
    for turn, packed in enumerate(refs[6:]):
        gate, up, down = refs[3 * turn : 3 * turn + 3]
        for j in range(packed.shape[0]):
            packed[j, :block, :unit] = gate[0, j * block : (j + 1) * block, :]
            packed[j, :block, unit:] = up[0, j * block : (j + 1) * block, :]
            packed[j, block:, :] = down[0, :, j * block : (j + 1) * block]


def pick_shards(kind, gate, up, down):
    depth, unit = gate.shape[1:]
    steps = 4
    each = depth // steps

    def specs(turn):
        def at(kind_ref):
            return kind_ref[0] if turn == 0 else 1 - kind_ref[0]

        tall = pl.BlockSpec((1, each, unit), lambda i, kind_ref: (at(kind_ref), i, 0))
        return [
            tall,
            tall,
            pl.BlockSpec((1, unit, each), lambda i, kind_ref: (at(kind_ref), 0, i)),
        ]

    packed = (depth // block, block + unit, block)
    out = pl.BlockSpec((each // block, *packed[1:]), lambda i, kind_ref: (i, 0, 0))
    return pl.pallas_call(
        pick_kernel,
        out_shape=(jax.ShapeDtypeStruct(packed, gate.dtype),) * 2,
        grid_spec=pltpu.PrefetchScalarGridSpec(
            num_scalar_prefetch=1, grid=(steps,), in_specs=specs(0) + specs(1), out_specs=(out, out)
        ),
        cost_estimate=pl.CostEstimate(flops=0, bytes_accessed=6 * 2**20, transcendentals=0),
    )(kind.reshape(1).astype(jnp.int32), gate, up, down, gate, up, down)


def ffn_kernel(count, place_ref, arrived, across, *refs):
    shards, added, (keep, give, hidden) = refs[:count], refs[count:-3], refs[-3:]
    row, core = place_ref[0], place_ref[1]
    f32 = jnp.float32
    rows, held = arrived.shape
    ring = held // block
    unit = block // 2

    def source(j, parity):
        return 2 * lax.rem(row - j + ring, ring) + parity

    def target(j, parity):
        return 2 * lax.rem(row + j, ring) + parity

    for k, shard in enumerate(shards):
        both = jnp.zeros((rows, block), f32)
        for j in range(ring):
            lanes = pl.ds(j * block, block)
            for part, parity in ((arrived, core), (across, 1 - core)):
                both += jnp.dot(
                    part[:, lanes], shard[source(j, parity), :block, :], preferred_element_type=f32
                )
        gate_val, up_val = both[:, :unit], both[:, unit:]
        silu = gate_val / (1.0 + jnp.exp(-gate_val))
        hidden[:, pl.ds(k * unit, unit)] = (silu * up_val).astype(hidden.dtype)
    for which, (parity, out) in enumerate(((core, keep), (1 - core, give))):
        for j in range(ring):
            lanes = pl.ds(j * block, block)
            total = added[which][:, lanes] if added else jnp.zeros((rows, block), f32)
            for k, shard in enumerate(shards):
                total += jnp.dot(
                    hidden[:, pl.ds(k * unit, unit)],
                    shard[target(j, parity), block:, :],
                    preferred_element_type=f32,
                )
            out[:, lanes] = total.astype(out.dtype)


def expert_rows(place, arrived, across, shards, added, give_type):
    rows, held = arrived.shape
    unit, width, count = block // 2, 2 * held, len(shards)
    whole = pl.BlockSpec(memory_space=pltpu.VMEM)
    return pl.pallas_call(
        functools.partial(ffn_kernel, count),
        out_shape=(
            jax.ShapeDtypeStruct((rows, held), jnp.float32),
            jax.ShapeDtypeStruct((rows, held), give_type),
        ),
        in_specs=[pl.BlockSpec(memory_space=pltpu.SMEM)] + [whole] * (2 + count + len(added)),
        out_specs=(whole, whole),
        scratch_shapes=[pltpu.VMEM((rows, count * unit), jnp.bfloat16)],
        compiler_params=pltpu.CompilerParams(vmem_limit_bytes=40 * 2**20),
        cost_estimate=pl.CostEstimate(
            flops=2 * rows * width * unit, bytes_accessed=2**20, transcendentals=0
        ),
    )(place, arrived, across, *shards, *added)


def on_device(tokens, norm_gain, router_logits, routes, gate_proj, up_proj, down_proj):
    bf16, f32 = jnp.bfloat16, jnp.float32
    ep_count = lax.axis_size("ep")
    row_count = lax.axis_size("x")
    group_size, width = tokens.shape
    local_experts = gate_proj.shape[0]
    top_count = routes.shape[1]
    expert_count = local_experts * ep_count
    capacity = 2 * group_size * top_count // expert_count
    share = capacity // (row_count // local_experts)
    core = lax.axis_index("core")
    row = lax.axis_index("x")
    kind = row // local_experts
    half = row % local_experts

    place = jnp.stack([row, core]).astype(jnp.int32)

    def ring_send(one, step):
        pairs = [(at, (at + step) % row_count) for at in range(row_count)]
        return lax.ppermute(one, "x", pairs)

    stacked = jnp.concatenate([tokens, jnp.broadcast_to(norm_gain[None, :], (16, width))], axis=0)
    parts = [stacked] + [ring_send(stacked, step) for step in range(1, row_count)]

    own, other = pick_shards(kind, gate_proj, up_proj, down_proj)
    parts, own, other = lax.optimization_barrier((parts, own, other))
    crossed = lax.ppermute(other, "x", cross_chip)
    near = lax.ppermute(own, "x", near_chip)
    crossed, near = lax.optimization_barrier((crossed, near))
    relayed = lax.ppermute(crossed, "x", near_chip)

    expert_iota = jnp.arange(expert_count, dtype=jnp.int32)
    hits = jnp.any(routes[:, :, None] == expert_iota[None, None, :], axis=1)
    earlier = jnp.tril(jnp.ones((group_size, group_size), bf16), -1)
    position = jnp.dot(earlier, hits.astype(bf16), preferred_element_type=f32)
    shifted = jnp.where(hits, router_logits, -jnp.inf)
    shifted = jnp.exp(shifted - jnp.max(shifted, axis=1, keepdims=True))
    gates = shifted / jnp.sum(shifted, axis=1, keepdims=True)

    def of_kind(table):
        return lax.dynamic_index_in_dim(
            table.reshape(group_size, ep_count, local_experts), kind, 2, keepdims=False
        )

    slot = jnp.where(of_kind(hits), of_kind(position), -1.0)
    gates = of_kind(gates)
    slot_iota = (jnp.arange(share, dtype=jnp.int32) + half * share).astype(f32)

    floated = [part[:group_size].astype(f32) for part in parts]
    squares = sum(jnp.sum(one * one, axis=1) for one in floated)[None, :]
    squares = squares + lax.ppermute(squares, "core", other_core)
    scale = lax.rsqrt(squares[0] / (width * row_count * chip_cores) + epsilon)[:, None]
    normed = jnp.concatenate(
        [
            (one * scale * part[group_size : group_size + 1].astype(f32)).astype(bf16)
            for one, part in zip(floated, parts)
        ],
        axis=1,
    )

    table = (slot.T[:, None, :] == slot_iota[None, :, None]).astype(bf16)
    outgoing = jnp.dot(
        table.reshape(ep_count * share, group_size), normed, preferred_element_type=f32
    ).astype(bf16)
    arrived = lax.all_to_all(
        outgoing.reshape(ep_count, share, -1), "ep", split_axis=0, concat_axis=0, tiled=True
    ).reshape(ep_count * share, -1)
    across = lax.ppermute(arrived, "core", other_core)
    added = expert_rows(place, arrived, across, (own, near, crossed), (), f32)
    keep, give = expert_rows(place, arrived, across, (relayed,), added, bf16)
    summed = keep + lax.ppermute(give, "core", other_core).astype(f32)
    returned = lax.all_to_all(
        summed.astype(bf16).reshape(ep_count, share, -1), "ep", split_axis=0, concat_axis=0, tiled=True
    ).reshape(ep_count * share, -1)

    weight = jnp.where(slot[:, :, None] == slot_iota[None, None, :], gates[:, :, None], 0.0)
    weight = weight.reshape(group_size, ep_count * share)
    high = lax.reduce_precision(weight, 8, 7)
    both = jnp.concatenate([high.astype(bf16), (weight - high).astype(bf16)], axis=0)
    mixed = jnp.dot(both, returned, preferred_element_type=f32)
    mixed = mixed[:group_size] + mixed[group_size:]

    result = mixed[:, :width]
    for step in range(1, row_count):
        result = result + ring_send(mixed[:, step * width : (step + 1) * width], step)
    return result.astype(bf16)


def solution(mesh):
    ep_count, tp_count = mesh.devices.shape
    fine = Mesh(
        mesh.devices.reshape(ep_count, tp_count // chip_cores, chip_cores), ("ep", "x", "core")
    )
    tp = ("x", "core")
    return jax.shard_map(
        on_device,
        mesh=fine,
        in_specs=(
            P("ep", tp),
            P(tp),
            P("ep", None),
            P("ep", None),
            P("ep", None, tp),
            P("ep", None, tp),
            P("ep", tp, None),
        ),
        out_specs=P("ep", tp),
        check_vma=False,
    )
```

```python
import functools
import jax
import jax.numpy as jnp
from jax import lax
from jax.experimental import pallas as pl
from jax.experimental.pallas import tpu as pltpu
from jax.sharding import Mesh, PartitionSpec as P

epsilon = 1e-05
chip_cores = 2
block = 256
other_core = [(0, 1), (1, 0)]
near_chip = [(0, 1), (1, 0), (2, 3), (3, 2)]
cross_chip = [(0, 3), (3, 0), (1, 2), (2, 1)]


def pick_kernel(kind_ref, gate, up, down, own, other, sems):
    unit = gate.shape[2]
    copies = []
    for turn, packed in enumerate((other, own)):
        at = kind_ref[0] if packed is own else 1 - kind_ref[0]
        for j in range(packed.shape[0]):
            wide = pl.ds(j * block, block)
            for source, target in (
                (gate.at[at, wide, :], packed.at[j, pl.ds(0, block), pl.ds(0, unit)]),
                (up.at[at, wide, :], packed.at[j, pl.ds(0, block), pl.ds(unit, unit)]),
                (down.at[at, :, wide], packed.at[j, pl.ds(block, unit), :]),
            ):
                copies.append(pltpu.make_async_copy(source, target, sems.at[len(copies)]))
    for copy in copies:
        copy.start()
    for copy in copies:
        copy.wait()


def pick_shards(kind, gate, up, down):
    depth, unit = gate.shape[1:]
    count = depth // block
    packed = jax.ShapeDtypeStruct((count, block + unit, block), gate.dtype)
    anywhere = pl.BlockSpec(memory_space=pl.ANY)
    whole = pl.BlockSpec(memory_space=pltpu.VMEM)
    return pl.pallas_call(
        pick_kernel,
        out_shape=(packed, packed),
        in_specs=[pl.BlockSpec(memory_space=pltpu.SMEM)] + [anywhere] * 3,
        out_specs=(whole, whole),
        scratch_shapes=[pltpu.SemaphoreType.DMA((6 * count,))],
        cost_estimate=pl.CostEstimate(flops=0, bytes_accessed=6 * 2**20, transcendentals=0),
    )(kind.reshape(1).astype(jnp.int32), gate, up, down)


def ffn_kernel(count, place_ref, arrived, across, *refs):
    lying, added, (keep, give, hidden, held_shards, sems) = refs[:count], refs[count:-5], refs[-5:]
    copies = [
        pltpu.make_async_copy(one, held_shards.at[k], sems.at[k]) for k, one in enumerate(lying)
    ]
    for copy in copies:
        copy.start()
    shards = [held_shards.at[k] for k in range(count)]
    row, core = place_ref[0], place_ref[1]
    f32 = jnp.float32
    rows, held = arrived.shape
    ring = held // block
    unit = block // 2

    def source(j, parity):
        return 2 * lax.rem(row - j + ring, ring) + parity

    def target(j, parity):
        return 2 * lax.rem(row + j, ring) + parity

    for k, shard in enumerate(shards):
        copies[k].wait()
        both = jnp.zeros((rows, block), f32)
        for j in range(ring):
            lanes = pl.ds(j * block, block)
            for part, parity in ((arrived, core), (across, 1 - core)):
                both += jnp.dot(
                    part[:, lanes], shard[source(j, parity), :block, :], preferred_element_type=f32
                )
        gate_val, up_val = both[:, :unit], both[:, unit:]
        silu = gate_val / (1.0 + jnp.exp(-gate_val))
        hidden[:, pl.ds(k * unit, unit)] = (silu * up_val).astype(hidden.dtype)
    for which, (parity, out) in enumerate(((core, keep), (1 - core, give))):
        for j in range(ring):
            lanes = pl.ds(j * block, block)
            total = added[which][:, lanes] if added else jnp.zeros((rows, block), f32)
            for k, shard in enumerate(shards):
                total += jnp.dot(
                    hidden[:, pl.ds(k * unit, unit)],
                    shard[target(j, parity), block:, :],
                    preferred_element_type=f32,
                )
            out[:, lanes] = total.astype(out.dtype)


def expert_rows(place, arrived, across, shards, added, give_type):
    rows, held = arrived.shape
    unit, width, count = block // 2, 2 * held, len(shards)
    whole = pl.BlockSpec(memory_space=pltpu.VMEM)
    return pl.pallas_call(
        functools.partial(ffn_kernel, count),
        out_shape=(
            jax.ShapeDtypeStruct((rows, held), jnp.float32),
            jax.ShapeDtypeStruct((rows, held), give_type),
        ),
        in_specs=[pl.BlockSpec(memory_space=pltpu.SMEM)]
        + [whole] * 2
        + [pl.BlockSpec(memory_space=pl.ANY)] * count
        + [whole] * len(added),
        out_specs=(whole, whole),
        scratch_shapes=[
            pltpu.VMEM((rows, count * unit), jnp.bfloat16),
            pltpu.VMEM((count, *shards[0].shape), jnp.bfloat16),
            pltpu.SemaphoreType.DMA((count,)),
        ],
        compiler_params=pltpu.CompilerParams(vmem_limit_bytes=40 * 2**20),
        cost_estimate=pl.CostEstimate(
            flops=2 * rows * width * unit, bytes_accessed=2**20, transcendentals=0
        ),
    )(place, arrived, across, *shards, *added)


def on_device(tokens, norm_gain, router_logits, routes, gate_proj, up_proj, down_proj):
    bf16, f32 = jnp.bfloat16, jnp.float32
    ep_count = lax.axis_size("ep")
    row_count = lax.axis_size("x")
    group_size, width = tokens.shape
    local_experts = gate_proj.shape[0]
    top_count = routes.shape[1]
    expert_count = local_experts * ep_count
    capacity = 2 * group_size * top_count // expert_count
    share = capacity // (row_count // local_experts)
    core = lax.axis_index("core")
    row = lax.axis_index("x")
    kind = row // local_experts
    half = row % local_experts

    place = jnp.stack([row, core]).astype(jnp.int32)

    def ring_send(one, step):
        pairs = [(at, (at + step) % row_count) for at in range(row_count)]
        return lax.ppermute(one, "x", pairs)

    padded = lax.pad(tokens, jnp.zeros((), bf16), [(0, 16, 0), (0, 0, 0)])
    at_row = lax.broadcasted_iota(jnp.int32, padded.shape, 0)
    stacked = jnp.where(at_row < group_size, padded, norm_gain[None, :])
    parts = [stacked] + [ring_send(stacked, step) for step in range(1, row_count)]

    own, other = pick_shards(kind, gate_proj, up_proj, down_proj)
    parts, own, other = lax.optimization_barrier((parts, own, other))
    crossed = lax.ppermute(other, "x", cross_chip)
    near = lax.ppermute(own, "x", near_chip)
    gated, _ = lax.optimization_barrier((crossed, near))
    relayed = lax.ppermute(gated, "x", near_chip)

    expert_iota = jnp.arange(expert_count, dtype=jnp.int32)
    hits = jnp.any(routes[:, :, None] == expert_iota[None, None, :], axis=1)
    earlier = jnp.tril(jnp.ones((group_size, group_size), bf16), -1)
    position = jnp.dot(earlier, hits.astype(bf16), preferred_element_type=f32)
    shifted = jnp.where(hits, router_logits, -jnp.inf)
    shifted = jnp.exp(shifted - jnp.max(shifted, axis=1, keepdims=True))
    gates = shifted / jnp.sum(shifted, axis=1, keepdims=True)

    def of_kind(table):
        return lax.dynamic_index_in_dim(
            table.reshape(group_size, ep_count, local_experts), kind, 2, keepdims=False
        )

    slot = jnp.where(of_kind(hits), of_kind(position), -1.0)
    gates = of_kind(gates)
    slot_iota = (jnp.arange(share, dtype=jnp.int32) + half * share).astype(f32)

    floated = [part[:group_size].astype(f32) for part in parts]
    squares = sum(jnp.sum(one * one, axis=1) for one in floated)[None, :]
    squares = squares + lax.ppermute(squares, "core", other_core)
    scale = lax.rsqrt(squares[0] / (width * row_count * chip_cores) + epsilon)[:, None]
    normed = jnp.concatenate(
        [
            (one * scale * part[group_size : group_size + 1].astype(f32)).astype(bf16)
            for one, part in zip(floated, parts)
        ],
        axis=1,
    )

    table = (slot.T[:, None, :] == slot_iota[None, :, None]).astype(bf16)
    outgoing = jnp.dot(
        table.reshape(ep_count * share, group_size), normed, preferred_element_type=f32
    ).astype(bf16)
    arrived = lax.all_to_all(
        outgoing.reshape(ep_count, share, -1), "ep", split_axis=0, concat_axis=0, tiled=True
    ).reshape(ep_count * share, -1)
    across = lax.ppermute(arrived, "core", other_core)
    added = expert_rows(place, arrived, across, (own, near, crossed), (), f32)
    keep, give = expert_rows(place, arrived, across, (relayed,), added, bf16)
    summed = keep + lax.ppermute(give, "core", other_core).astype(f32)
    returned = lax.all_to_all(
        summed.astype(bf16).reshape(ep_count, share, -1), "ep", split_axis=0, concat_axis=0, tiled=True
    ).reshape(ep_count * share, -1)

    weight = jnp.where(slot[:, :, None] == slot_iota[None, None, :], gates[:, :, None], 0.0)
    weight = weight.reshape(group_size, ep_count * share)
    high = lax.reduce_precision(weight, 8, 7)
    both = jnp.concatenate([high.astype(bf16), (weight - high).astype(bf16)], axis=0)
    mixed = jnp.dot(both, returned, preferred_element_type=f32)
    mixed = mixed[:group_size] + mixed[group_size:]

    result = mixed[:, :width]
    for step in range(1, row_count):
        result = result + ring_send(mixed[:, step * width : (step + 1) * width], step)
    return result.astype(bf16)


def solution(mesh):
    ep_count, tp_count = mesh.devices.shape
    fine = Mesh(
        mesh.devices.reshape(ep_count, tp_count // chip_cores, chip_cores), ("ep", "x", "core")
    )
    tp = ("x", "core")
    return jax.shard_map(
        on_device,
        mesh=fine,
        in_specs=(
            P("ep", tp),
            P(tp),
            P("ep", None),
            P("ep", None),
            P("ep", None, tp),
            P("ep", None, tp),
            P("ep", tp, None),
        ),
        out_specs=P("ep", tp),
        check_vma=False,
    )
```

```python
import functools
import jax
import jax.numpy as jnp
from jax import lax
from jax.experimental import pallas as pl
from jax.experimental.pallas import tpu as pltpu
from jax.sharding import Mesh, PartitionSpec as P

epsilon = 1e-05
chip_cores = 2
block = 256
other_core = [(0, 1), (1, 0)]
detoured = 2


def row_pairs(partner, lent=False):
    pairs = []
    for parity in range(2):
        turn = 1 - parity if lent else parity
        for part in range(4):
            source, target = (part + turn) % 4, (partner(part) + turn) % 4
            pairs.append((4 * parity + source, 4 * parity + target))
    return pairs


near_chip = row_pairs(lambda part: part ^ 1)
near_lent = row_pairs(lambda part: part ^ 1, True)
cross_chip = row_pairs(lambda part: 3 - part)
other_row = [(at, (at + 4) % 8) for at in range(8)]


def pick_kernel(kind_ref, gate, up, down, *refs):
    pieces, sems = refs[:-1], refs[-1]
    unit = gate.shape[2]
    copies = []
    first = 0
    for turn, packed in enumerate(pieces):
        first = 0 if turn in (0, 2) else first
        at = 1 - kind_ref[0] if turn < 2 else kind_ref[0]
        for j in range(packed.shape[0]):
            wide = pl.ds((first + j) * block, block)
            for source, target in (
                (gate.at[at, wide, :], packed.at[j, pl.ds(0, block), pl.ds(0, unit)]),
                (up.at[at, wide, :], packed.at[j, pl.ds(0, block), pl.ds(unit, unit)]),
                (down.at[at, :, wide], packed.at[j, pl.ds(block, unit), :]),
            ):
                copies.append(pltpu.make_async_copy(source, target, sems.at[len(copies)]))
        first += packed.shape[0]
    for copy in copies:
        copy.start()
    for copy in copies:
        copy.wait()


def pick_shards(kind, gate, up, down):
    depth, unit = gate.shape[1:]
    count = depth // block
    anywhere = pl.BlockSpec(memory_space=pl.ANY)
    whole = pl.BlockSpec(memory_space=pltpu.VMEM)
    other = [count - detoured, detoured]
    own = [count - detoured, detoured]
    picked = pl.pallas_call(
        pick_kernel,
        out_shape=tuple(
            jax.ShapeDtypeStruct((size, block + unit, block), gate.dtype) for size in other + own
        ),
        in_specs=[pl.BlockSpec(memory_space=pltpu.SMEM)] + [anywhere] * 3,
        out_specs=(whole,) * 4,
        scratch_shapes=[pltpu.SemaphoreType.DMA((6 * count,))],
        cost_estimate=pl.CostEstimate(flops=0, bytes_accessed=6 * 2**20, transcendentals=0),
    )(kind.reshape(1).astype(jnp.int32), gate, up, down)
    return picked[:2], picked[2:]


def ffn_kernel(count, place_ref, arrived, across, *refs):
    lying, added, (keep, give, hidden, held_shards, sems) = refs[:count], refs[count:-5], refs[-5:]
    total_blocks = held_shards.shape[1]
    copies, first = [], 0
    for n, piece in enumerate(lying):
        into = held_shards.at[first // total_blocks, pl.ds(first % total_blocks, piece.shape[0])]
        copies.append((first // total_blocks, pltpu.make_async_copy(piece, into, sems.at[n])))
        first += piece.shape[0]
    for _, copy in copies:
        copy.start()
    shards = [held_shards.at[k] for k in range(held_shards.shape[0])]
    row, core = place_ref[0], place_ref[1]
    f32 = jnp.float32
    rows, held = arrived.shape
    ring = held // block
    unit = block // 2

    def source(j, parity):
        return 2 * lax.rem(row - j + ring, ring) + parity

    def target(j, parity):
        return 2 * lax.rem(row + j, ring) + parity

    for k, shard in enumerate(shards):
        for shard_of, copy in copies:
            if shard_of == k:
                copy.wait()
        both = jnp.zeros((rows, block), f32)
        for j in range(ring):
            lanes = pl.ds(j * block, block)
            for part, parity in ((arrived, core), (across, 1 - core)):
                both += jnp.dot(
                    part[:, lanes], shard[source(j, parity), :block, :], preferred_element_type=f32
                )
        gate_val, up_val = both[:, :unit], both[:, unit:]
        silu = gate_val / (1.0 + jnp.exp(-gate_val))
        hidden[:, pl.ds(k * unit, unit)] = (silu * up_val).astype(hidden.dtype)
    for which, (parity, out) in enumerate(((core, keep), (1 - core, give))):
        for j in range(ring):
            lanes = pl.ds(j * block, block)
            total = added[which][:, lanes] if added else jnp.zeros((rows, block), f32)
            down = jnp.concatenate([shard[target(j, parity), block:, :] for shard in shards], axis=0)
            total += jnp.dot(hidden[...], down, preferred_element_type=f32)
            out[:, lanes] = total.astype(out.dtype)


def expert_rows(place, arrived, across, pieces, added, give_type):
    rows, held = arrived.shape
    unit, width, count = block // 2, 2 * held, len(pieces)
    blocks = width // block
    shards = sum(piece.shape[0] for piece in pieces) // blocks
    whole = pl.BlockSpec(memory_space=pltpu.VMEM)
    return pl.pallas_call(
        functools.partial(ffn_kernel, count),
        out_shape=(
            jax.ShapeDtypeStruct((rows, held), jnp.float32),
            jax.ShapeDtypeStruct((rows, held), give_type),
        ),
        in_specs=[pl.BlockSpec(memory_space=pltpu.SMEM)]
        + [whole] * 2
        + [pl.BlockSpec(memory_space=pl.ANY)] * count
        + [whole] * len(added),
        out_specs=(whole, whole),
        scratch_shapes=[
            pltpu.VMEM((rows, shards * unit), jnp.bfloat16),
            pltpu.VMEM((shards, blocks, *pieces[0].shape[1:]), jnp.bfloat16),
            pltpu.SemaphoreType.DMA((count,)),
        ],
        compiler_params=pltpu.CompilerParams(vmem_limit_bytes=40 * 2**20),
        cost_estimate=pl.CostEstimate(
            flops=2 * rows * width * unit, bytes_accessed=2**20, transcendentals=0
        ),
    )(place, arrived, across, *pieces, *added)


def on_device(tokens, norm_gain, router_logits, routes, gate_proj, up_proj, down_proj):
    bf16, f32 = jnp.bfloat16, jnp.float32
    ep = ("line", "pair")
    ep_count = lax.axis_size(ep)
    row_count = lax.axis_size("x")
    group_size, width = tokens.shape
    local_experts = gate_proj.shape[0]
    top_count = routes.shape[1]
    expert_count = local_experts * ep_count
    capacity = 2 * group_size * top_count // expert_count
    share = capacity // (row_count // local_experts)
    core = lax.axis_index("core")
    row = lax.axis_index("x")
    split = row_count // local_experts
    part = (row - lax.axis_index("pair")) % row_count
    peers = (row - jnp.arange(ep_count, dtype=jnp.int32) % 2) % row_count

    place = jnp.stack([row, core]).astype(jnp.int32)

    def ring_send(one, step):
        pairs = [(at, (at + step) % row_count) for at in range(row_count)]
        return lax.ppermute(one, "x", pairs)

    padded = lax.pad(tokens, jnp.zeros((), bf16), [(0, 16, 0), (0, 0, 0)])
    at_row = lax.broadcasted_iota(jnp.int32, padded.shape, 0)
    stacked = jnp.where(at_row < group_size, padded, norm_gain[None, :])
    parts = [stacked] + [ring_send(stacked, step) for step in range(1, row_count)]

    other, own = pick_shards(part // split, gate_proj, up_proj, down_proj)
    parts, own, other = lax.optimization_barrier((parts, own, other))

    def send(one, pairs):
        return lax.ppermute(one, ("pair", "x"), pairs)

    def after(one, *others):
        return lax.optimization_barrier((one, *others))[0]

    crossed = [send(other[0], cross_chip)]
    near = send(own[0], near_chip)
    crossed.append(send(after(other[1], crossed[0]), cross_chip))
    relayed = [send(after(crossed[0], near), near_chip)]
    relayed.append(send(after(crossed[1], relayed[0]), near_chip))
    passed = send(after(send(own[1], other_row), crossed[1]), near_lent)
    lent = send(passed, other_row)

    expert_iota = jnp.arange(expert_count, dtype=jnp.int32)
    hits = jnp.any(routes[:, :, None] == expert_iota[None, None, :], axis=1)
    earlier = jnp.tril(jnp.ones((group_size, group_size), bf16), -1)
    position = jnp.dot(earlier, hits.astype(bf16), preferred_element_type=f32)
    shifted = jnp.where(hits, router_logits, -jnp.inf)
    shifted = jnp.exp(shifted - jnp.max(shifted, axis=1, keepdims=True))
    gates = shifted / jnp.sum(shifted, axis=1, keepdims=True)

    def of_kind(table):
        table = table.reshape(group_size, ep_count, local_experts)
        return jnp.where((peers // split == 0)[None, :], table[:, :, 0], table[:, :, 1])

    slot = jnp.where(of_kind(hits), of_kind(position), -1.0)
    slot = slot - (peers % split * share).astype(f32)[None, :]
    gates = of_kind(gates)
    slot_iota = jnp.arange(share, dtype=jnp.int32).astype(f32)

    floated = [part[:group_size].astype(f32) for part in parts]
    squares = sum(jnp.sum(one * one, axis=1) for one in floated)[None, :]
    squares = squares + lax.ppermute(squares, "core", other_core)
    scale = lax.rsqrt(squares[0] / (width * row_count * chip_cores) + epsilon)[:, None]
    normed = jnp.concatenate(
        [
            (one * scale * part[group_size : group_size + 1].astype(f32)).astype(bf16)
            for one, part in zip(floated, parts)
        ],
        axis=1,
    )

    table = (slot.T[:, None, :] == slot_iota[None, :, None]).astype(bf16)
    outgoing = jnp.dot(
        table.reshape(ep_count * share, group_size), normed, preferred_element_type=f32
    ).astype(bf16)
    arrived = lax.all_to_all(
        outgoing.reshape(ep_count, share, -1), ep, split_axis=0, concat_axis=0, tiled=True
    ).reshape(ep_count * share, -1)
    arrived = after(arrived, relayed[0], passed)
    across = lax.ppermute(arrived, "core", other_core)
    added = expert_rows(place, arrived, across, (*own, *crossed), (), f32)
    keep, give = expert_rows(place, arrived, across, (near, lent, *relayed), added, bf16)
    summed = keep + lax.ppermute(give, "core", other_core).astype(f32)
    returned = lax.all_to_all(
        summed.astype(bf16).reshape(ep_count, share, -1), ep, split_axis=0, concat_axis=0, tiled=True
    ).reshape(ep_count * share, -1)

    weight = jnp.where(slot[:, :, None] == slot_iota[None, None, :], gates[:, :, None], 0.0)
    weight = weight.reshape(group_size, ep_count * share)
    high = lax.reduce_precision(weight, 8, 7)
    both = jnp.concatenate([high.astype(bf16), (weight - high).astype(bf16)], axis=0)
    mixed = jnp.dot(both, returned, preferred_element_type=f32)
    mixed = mixed[:group_size] + mixed[group_size:]

    result = mixed[:, :width]
    for step in range(1, row_count):
        sent = mixed[:, step * width : (step + 1) * width].astype(bf16)
        result = result + ring_send(sent, step).astype(f32)
    return result.astype(bf16)


def solution(mesh):
    ep_count, tp_count = mesh.devices.shape
    fine = Mesh(
        mesh.devices.reshape(ep_count // 2, 2, tp_count // chip_cores, chip_cores),
        ("line", "pair", "x", "core"),
    )
    ep, tp = ("line", "pair"), ("x", "core")
    return jax.shard_map(
        on_device,
        mesh=fine,
        in_specs=(
            P(ep, tp),
            P(tp),
            P(ep, None),
            P(ep, None),
            P(ep, None, tp),
            P(ep, None, tp),
            P(ep, tp, None),
        ),
        out_specs=P(ep, tp),
        check_vma=False,
    )
```

```python
import functools
import jax
import jax.numpy as jnp
from jax import lax
from jax.experimental import pallas as pl
from jax.experimental.pallas import tpu as pltpu
from jax.sharding import Mesh, PartitionSpec as P

epsilon = 1e-05
chip_cores = 2
block = 256
other_core = [(0, 1), (1, 0)]
detoured = 2


def row_pairs(partner, lent=False):
    pairs = []
    for parity in range(2):
        turn = 1 - parity if lent else parity
        for part in range(4):
            source, target = (part + turn) % 4, (partner(part) + turn) % 4
            pairs.append((4 * parity + source, 4 * parity + target))
    return pairs


near_chip = row_pairs(lambda part: part ^ 1)
near_lent = row_pairs(lambda part: part ^ 1, True)
cross_chip = row_pairs(lambda part: 3 - part)
other_row = [(at, (at + 4) % 8) for at in range(8)]


def pick_kernel(kind_ref, gate, up, down, *refs):
    pieces, sems = refs[:-1], refs[-1]
    unit = gate.shape[2]
    copies = []
    first = 0
    for turn, packed in enumerate(pieces):
        first = 0 if turn in (0, 2) else first
        at = 1 - kind_ref[0] if turn < 2 else kind_ref[0]
        for j in range(packed.shape[0]):
            wide = pl.ds((first + j) * block, block)
            for source, target in (
                (gate.at[at, wide, :], packed.at[j, pl.ds(0, block), pl.ds(0, unit)]),
                (up.at[at, wide, :], packed.at[j, pl.ds(0, block), pl.ds(unit, unit)]),
                (down.at[at, :, wide], packed.at[j, pl.ds(block, unit), :]),
            ):
                copies.append(pltpu.make_async_copy(source, target, sems.at[len(copies)]))
        first += packed.shape[0]
    for copy in copies:
        copy.start()
    for copy in copies:
        copy.wait()


def pick_shards(kind, gate, up, down):
    depth, unit = gate.shape[1:]
    count = depth // block
    anywhere = pl.BlockSpec(memory_space=pl.ANY)
    whole = pl.BlockSpec(memory_space=pltpu.VMEM)
    other = [count - detoured, detoured]
    own = [count - detoured, detoured]
    picked = pl.pallas_call(
        pick_kernel,
        out_shape=tuple(
            jax.ShapeDtypeStruct((size, block + unit, block), gate.dtype) for size in other + own
        ),
        in_specs=[pl.BlockSpec(memory_space=pltpu.SMEM)] + [anywhere] * 3,
        out_specs=(whole,) * 4,
        scratch_shapes=[pltpu.SemaphoreType.DMA((6 * count,))],
        cost_estimate=pl.CostEstimate(flops=0, bytes_accessed=6 * 2**20, transcendentals=0),
    )(kind.reshape(1).astype(jnp.int32), gate, up, down)
    return picked[:2], picked[2:]


def ffn_kernel(sizes, place_ref, arrived, across, *refs):
    pieces, added = refs[: len(sizes)], refs[len(sizes) : -6]
    keep, give, joined, downs, hidden, sems = refs[-6:]
    row, core = place_ref[0], place_ref[1]
    f32 = jnp.float32
    held = arrived.shape[1]
    ring = held // block
    unit = block // 2

    copies, first = [], 0
    for piece, size in zip(pieces, sizes):
        for j in range(size):
            k, i = divmod(first + j, 2 * ring)
            mine = lax.rem(i % 2 + core, 2)
            source = mine * ring + lax.rem(row - i // 2 + ring, ring)
            target = lax.rem(i // 2 - row + ring, ring)
            gate_up = joined.at[k, source]
            lanes = pl.ds(pl.multiple_of(target * block, block), block)
            down = downs.at[mine, pl.ds(k * unit, unit), lanes]
            for turn, (part, into) in enumerate(
                ((piece.at[j, pl.ds(0, block)], gate_up), (piece.at[j, pl.ds(block, unit)], down))
            ):
                sem = sems.at[2 * (first + j) + turn]
                copies.append((k, turn, pltpu.make_async_copy(part, into, sem)))
        first += size
    for turn in range(2):
        for _, when, copy in copies:
            if when == turn:
                copy.start()

    for k in range(joined.shape[0]):
        for shard_of, turn, copy in copies:
            if shard_of == k and turn == 0:
                copy.wait()
        mine = joined[k, :ring].reshape(held, block)
        theirs = joined[k, ring:].reshape(held, block)
        both = jnp.dot(arrived[...], mine, preferred_element_type=f32)
        both += jnp.dot(across[...], theirs, preferred_element_type=f32)
        gate_val, up_val = both[:, :unit], both[:, unit:]
        silu = gate_val / (1.0 + jnp.exp(-gate_val))
        hidden[:, pl.ds(k * unit, unit)] = (silu * up_val).astype(hidden.dtype)
    for _, turn, copy in copies:
        if turn == 1:
            copy.wait()
    for which, out in enumerate((keep, give)):
        total = jnp.dot(hidden[...], downs[which], preferred_element_type=f32)
        if added:
            total += added[which][...]
        out[...] = total.astype(out.dtype)


def expert_rows(place, arrived, across, pieces, added, give_type):
    rows, held = arrived.shape
    unit, width = block // 2, 2 * held
    sizes = tuple(piece.shape[0] for piece in pieces)
    blocks = width // block
    shards = sum(sizes) // blocks
    whole = pl.BlockSpec(memory_space=pltpu.VMEM)
    return pl.pallas_call(
        functools.partial(ffn_kernel, sizes),
        out_shape=(
            jax.ShapeDtypeStruct((rows, held), jnp.float32),
            jax.ShapeDtypeStruct((rows, held), give_type),
        ),
        in_specs=[pl.BlockSpec(memory_space=pltpu.SMEM)]
        + [whole] * 2
        + [pl.BlockSpec(memory_space=pl.ANY)] * len(sizes)
        + [whole] * len(added),
        out_specs=(whole, whole),
        scratch_shapes=[
            pltpu.VMEM((shards, blocks, block, block), jnp.bfloat16),
            pltpu.VMEM((2, shards * unit, held), jnp.bfloat16),
            pltpu.VMEM((rows, shards * unit), jnp.bfloat16),
            pltpu.SemaphoreType.DMA((2 * shards * blocks,)),
        ],
        compiler_params=pltpu.CompilerParams(vmem_limit_bytes=40 * 2**20),
        cost_estimate=pl.CostEstimate(
            flops=2 * rows * width * unit, bytes_accessed=2**20, transcendentals=0
        ),
    )(place, arrived, across, *pieces, *added)


def on_device(tokens, norm_gain, router_logits, routes, gate_proj, up_proj, down_proj):
    bf16, f32 = jnp.bfloat16, jnp.float32
    ep = ("line", "pair")
    ep_count = lax.axis_size(ep)
    row_count = lax.axis_size("x")
    group_size, width = tokens.shape
    local_experts = gate_proj.shape[0]
    top_count = routes.shape[1]
    expert_count = local_experts * ep_count
    capacity = 2 * group_size * top_count // expert_count
    share = capacity // (row_count // local_experts)
    core = lax.axis_index("core")
    row = lax.axis_index("x")
    split = row_count // local_experts
    part = (row - lax.axis_index("pair")) % row_count
    peers = (row - jnp.arange(ep_count, dtype=jnp.int32) % 2) % row_count

    place = jnp.stack([row, core]).astype(jnp.int32)

    def ring_send(one, step):
        pairs = [(at, (at + step) % row_count) for at in range(row_count)]
        return lax.ppermute(one, "x", pairs)

    padded = lax.pad(tokens, jnp.zeros((), bf16), [(0, 16, 0), (0, 0, 0)])
    at_row = lax.broadcasted_iota(jnp.int32, padded.shape, 0)
    stacked = jnp.where(at_row < group_size, padded, norm_gain[None, :])
    parts = [stacked] + [ring_send(stacked, step) for step in range(1, row_count)]

    other, own = pick_shards(part // split, gate_proj, up_proj, down_proj)
    parts, own, other = lax.optimization_barrier((parts, own, other))

    def send(one, pairs):
        return lax.ppermute(one, ("pair", "x"), pairs)

    def after(one, *others):
        return lax.optimization_barrier((one, *others))[0]

    crossed = [send(other[0], cross_chip)]
    near = send(own[0], near_chip)
    crossed.append(send(after(other[1], crossed[0]), cross_chip))
    relayed = [send(after(crossed[0], near), near_chip)]
    relayed.append(send(after(crossed[1], relayed[0]), near_chip))
    passed = send(after(send(own[1], other_row), crossed[1]), near_lent)
    lent = send(passed, other_row)

    routes = after(routes, own[0])

    expert_iota = jnp.arange(expert_count, dtype=jnp.int32)
    hits = jnp.any(routes[:, :, None] == expert_iota[None, None, :], axis=1)
    earlier = jnp.tril(jnp.ones((group_size, group_size), bf16), -1)
    position = jnp.dot(earlier, hits.astype(bf16), preferred_element_type=f32)

    def of_kind(table):
        table = table.reshape(group_size, ep_count, local_experts)
        return jnp.where((peers // split == 0)[None, :], table[:, :, 0], table[:, :, 1])

    slot = jnp.where(of_kind(hits), of_kind(position), -1.0)
    slot = slot - (peers % split * share).astype(f32)[None, :]
    slot_iota = jnp.arange(share, dtype=jnp.int32).astype(f32)

    floated = [part[:group_size].astype(f32) for part in parts]
    squares = sum(jnp.sum(one * one, axis=1) for one in floated)[None, :]
    squares = squares + lax.ppermute(squares, "core", other_core)
    scale = lax.rsqrt(squares[0] / (width * row_count * chip_cores) + epsilon)[:, None]
    normed = jnp.concatenate(
        [
            (one * scale * part[group_size : group_size + 1].astype(f32)).astype(bf16)
            for one, part in zip(floated, parts)
        ],
        axis=1,
    )

    table = (slot.T[:, None, :] == slot_iota[None, :, None]).astype(bf16)
    outgoing = jnp.dot(
        table.reshape(ep_count * share, group_size), normed, preferred_element_type=f32
    ).astype(bf16)
    arrived = lax.all_to_all(
        outgoing.reshape(ep_count, share, -1), ep, split_axis=0, concat_axis=0, tiled=True
    ).reshape(ep_count * share, -1)
    arrived = after(arrived, relayed[0], passed)
    across = lax.ppermute(arrived, "core", other_core)
    added = expert_rows(place, arrived, across, (*own, *crossed), (), f32)
    keep, give = expert_rows(place, arrived, across, (near, lent, *relayed), added, bf16)
    summed = keep + lax.ppermute(give, "core", other_core).astype(f32)
    returned = lax.all_to_all(
        summed.astype(bf16).reshape(ep_count, share, -1), ep, split_axis=0, concat_axis=0, tiled=True
    ).reshape(ep_count * share, -1)

    shifted = jnp.where(hits, after(router_logits, arrived), -jnp.inf)
    shifted = jnp.exp(shifted - jnp.max(shifted, axis=1, keepdims=True))
    gates = of_kind(shifted / jnp.sum(shifted, axis=1, keepdims=True))
    weight = jnp.where(slot[:, :, None] == slot_iota[None, None, :], gates[:, :, None], 0.0)
    weight = weight.reshape(group_size, ep_count * share)
    high = lax.reduce_precision(weight, 8, 7)
    both = jnp.concatenate([high.astype(bf16), (weight - high).astype(bf16)], axis=0)
    mixed = jnp.dot(both, returned, preferred_element_type=f32)
    mixed = mixed[:group_size] + mixed[group_size:]

    result = mixed[:, :width]
    for step in range(1, row_count):
        sent = mixed[:, step * width : (step + 1) * width].astype(bf16)
        result = result + ring_send(sent, step).astype(f32)
    return result.astype(bf16)


def solution(mesh):
    ep_count, tp_count = mesh.devices.shape
    fine = Mesh(
        mesh.devices.reshape(ep_count // 2, 2, tp_count // chip_cores, chip_cores),
        ("line", "pair", "x", "core"),
    )
    ep, tp = ("line", "pair"), ("x", "core")
    return jax.shard_map(
        on_device,
        mesh=fine,
        in_specs=(
            P(ep, tp),
            P(tp),
            P(ep, None),
            P(ep, None),
            P(ep, None, tp),
            P(ep, None, tp),
            P(ep, tp, None),
        ),
        out_specs=P(ep, tp),
        check_vma=False,
    )
```

```python
import functools
import jax
import jax.numpy as jnp
from jax import lax
from jax.experimental import pallas as pl
from jax.experimental.pallas import tpu as pltpu
from jax.sharding import Mesh, PartitionSpec as P

epsilon = 1e-05
chip_cores = 2
block = 256
other_core = [(0, 1), (1, 0)]
detoured = 2


def row_pairs(partner, lent=False):
    pairs = []
    for parity in range(2):
        turn = 1 - parity if lent else parity
        for part in range(4):
            source, target = (part + turn) % 4, (partner(part) + turn) % 4
            pairs.append((4 * parity + source, 4 * parity + target))
    return pairs


near_chip = row_pairs(lambda part: part ^ 1)
near_lent = row_pairs(lambda part: part ^ 1, True)
cross_chip = row_pairs(lambda part: 3 - part)
other_row = [(at, (at + 4) % 8) for at in range(8)]


def pick_kernel(kind_ref, gate, up, down, *refs):
    pieces, sems = refs[:-1], refs[-1]
    unit = gate.shape[2]
    copies = []
    first = 0
    for turn, packed in enumerate(pieces):
        first = 0 if turn in (0, 2) else first
        at = 1 - kind_ref[0] if turn < 2 else kind_ref[0]
        for j in range(packed.shape[0]):
            wide = pl.ds((first + j) * block, block)
            for source, target in (
                (gate.at[at, wide, :], packed.at[j, pl.ds(0, block), pl.ds(0, unit)]),
                (up.at[at, wide, :], packed.at[j, pl.ds(0, block), pl.ds(unit, unit)]),
                (down.at[at, :, wide], packed.at[j, pl.ds(block, unit), :]),
            ):
                copies.append(pltpu.make_async_copy(source, target, sems.at[len(copies)]))
        first += packed.shape[0]
    for copy in copies:
        copy.start()
    for copy in copies:
        copy.wait()


def pick_shards(kind, gate, up, down):
    depth, unit = gate.shape[1:]
    count = depth // block
    anywhere = pl.BlockSpec(memory_space=pl.ANY)
    whole = pl.BlockSpec(memory_space=pltpu.VMEM)
    other = [count - detoured, detoured]
    own = [count - detoured, detoured]
    picked = pl.pallas_call(
        pick_kernel,
        out_shape=tuple(
            jax.ShapeDtypeStruct((size, block + unit, block), gate.dtype) for size in other + own
        ),
        in_specs=[pl.BlockSpec(memory_space=pltpu.SMEM)] + [anywhere] * 3,
        out_specs=(whole,) * 4,
        scratch_shapes=[pltpu.SemaphoreType.DMA((6 * count,))],
        cost_estimate=pl.CostEstimate(flops=0, bytes_accessed=6 * 2**20, transcendentals=0),
    )(kind.reshape(1).astype(jnp.int32), gate, up, down)
    return picked[:2], picked[2:]


def ffn_kernel(count, place_ref, arrived, across, *refs):
    lying, (keep, give, hidden, held_shards, sems) = refs[:count], refs[count:]
    total_blocks = held_shards.shape[1]
    copies, first = [], 0
    for n, piece in enumerate(lying):
        into = held_shards.at[first // total_blocks, pl.ds(first % total_blocks, piece.shape[0])]
        copies.append((first // total_blocks, pltpu.make_async_copy(piece, into, sems.at[n])))
        first += piece.shape[0]
    for _, copy in copies:
        copy.start()
    shards = [held_shards.at[k] for k in range(held_shards.shape[0])]
    row, core = place_ref[0], place_ref[1]
    f32 = jnp.float32
    rows, held = arrived.shape
    ring = held // block
    unit = block // 2

    def source(j, parity):
        return 2 * lax.rem(row - j + ring, ring) + parity

    def target(j, parity):
        return 2 * lax.rem(row + j, ring) + parity

    for k, shard in enumerate(shards):
        for shard_of, copy in copies:
            if shard_of == k:
                copy.wait()
        both = jnp.zeros((rows, block), f32)
        for j in range(ring):
            lanes = pl.ds(j * block, block)
            for part, parity in ((arrived, core), (across, 1 - core)):
                both += jnp.dot(
                    part[:, lanes], shard[source(j, parity), :block, :], preferred_element_type=f32
                )
        gate_val, up_val = both[:, :unit], both[:, unit:]
        silu = gate_val / (1.0 + jnp.exp(-gate_val))
        hidden[:, pl.ds(k * unit, unit)] = (silu * up_val).astype(hidden.dtype)
    for parity, out in ((core, keep), (1 - core, give)):
        for j in range(ring):
            lanes = pl.ds(j * block, block)
            down = jnp.concatenate([shard[target(j, parity), block:, :] for shard in shards], axis=0)
            total = jnp.dot(hidden[...], down, preferred_element_type=f32)
            out[:, lanes] = total.astype(out.dtype)


def expert_rows(place, arrived, across, pieces):
    rows, held = arrived.shape
    unit, width, count = block // 2, 2 * held, len(pieces)
    blocks = width // block
    shards = sum(piece.shape[0] for piece in pieces) // blocks
    whole = pl.BlockSpec(memory_space=pltpu.VMEM)
    return pl.pallas_call(
        functools.partial(ffn_kernel, count),
        out_shape=(
            jax.ShapeDtypeStruct((rows, held), jnp.float32),
            jax.ShapeDtypeStruct((rows, held), jnp.bfloat16),
        ),
        in_specs=[pl.BlockSpec(memory_space=pltpu.SMEM)]
        + [whole] * 2
        + [pl.BlockSpec(memory_space=pl.ANY)] * count,
        out_specs=(whole, whole),
        scratch_shapes=[
            pltpu.VMEM((rows, shards * unit), jnp.bfloat16),
            pltpu.VMEM((shards, blocks, *pieces[0].shape[1:]), jnp.bfloat16),
            pltpu.SemaphoreType.DMA((count,)),
        ],
        compiler_params=pltpu.CompilerParams(vmem_limit_bytes=40 * 2**20),
        cost_estimate=pl.CostEstimate(
            flops=2 * rows * width * unit, bytes_accessed=2**20, transcendentals=0
        ),
    )(place, arrived, across, *pieces)


def on_device(tokens, norm_gain, router_logits, routes, gate_proj, up_proj, down_proj):
    bf16, f32 = jnp.bfloat16, jnp.float32
    ep = ("line", "pair")
    ep_count = lax.axis_size(ep)
    row_count = lax.axis_size("x")
    group_size, width = tokens.shape
    local_experts = gate_proj.shape[0]
    top_count = routes.shape[1]
    expert_count = local_experts * ep_count
    capacity = 2 * group_size * top_count // expert_count
    share = capacity // (row_count // local_experts)
    core = lax.axis_index("core")
    row = lax.axis_index("x")
    split = row_count // local_experts
    part = (row - lax.axis_index("pair")) % row_count
    peers = (row - jnp.arange(ep_count, dtype=jnp.int32) % 2) % row_count

    place = jnp.stack([row, core]).astype(jnp.int32)

    def ring_send(one, step):
        pairs = [(at, (at + step) % row_count) for at in range(row_count)]
        return lax.ppermute(one, "x", pairs)

    padded = lax.pad(tokens, jnp.zeros((), bf16), [(0, 16, 0), (0, 0, 0)])
    at_row = lax.broadcasted_iota(jnp.int32, padded.shape, 0)
    stacked = jnp.where(at_row < group_size, padded, norm_gain[None, :])
    parts = [stacked] + [ring_send(stacked, step) for step in range(1, row_count)]

    other, own = pick_shards(part // split, gate_proj, up_proj, down_proj)
    parts, own, other = lax.optimization_barrier((parts, own, other))

    def send(one, pairs):
        return lax.ppermute(one, ("pair", "x"), pairs)

    def after(one, *others):
        return lax.optimization_barrier((one, *others))[0]

    crossed = [send(other[0], cross_chip)]
    near = send(own[0], near_chip)
    passed = after(send(own[1], other_row), crossed[0], near)
    passed = send(passed, near_lent)
    crossed.append(send(after(other[1], passed), cross_chip))
    lent = send(passed, other_row)
    relayed = [send(after(crossed[0], near), near_chip), send(crossed[1], near_chip)]

    routes = after(routes, own[0])

    expert_iota = jnp.arange(expert_count, dtype=jnp.int32)
    hits = jnp.any(routes[:, :, None] == expert_iota[None, None, :], axis=1)
    earlier = jnp.tril(jnp.ones((group_size, group_size), bf16), -1)
    position = jnp.dot(earlier, hits.astype(bf16), preferred_element_type=f32)

    def of_kind(table):
        table = table.reshape(group_size, ep_count, local_experts)
        return jnp.where((peers // split == 0)[None, :], table[:, :, 0], table[:, :, 1])

    slot = jnp.where(of_kind(hits), of_kind(position), -1.0)
    slot = slot - (peers % split * share).astype(f32)[None, :]
    slot_iota = jnp.arange(share, dtype=jnp.int32).astype(f32)

    floated = [part[:group_size].astype(f32) for part in parts]
    squares = sum(jnp.sum(one * one, axis=1) for one in floated)[None, :]
    squares = squares + lax.ppermute(squares, "core", other_core)
    scale = lax.rsqrt(squares[0] / (width * row_count * chip_cores) + epsilon)[:, None]
    normed = jnp.concatenate(
        [
            (one * scale * part[group_size : group_size + 1].astype(f32)).astype(bf16)
            for one, part in zip(floated, parts)
        ],
        axis=1,
    )

    table = (slot.T[:, None, :] == slot_iota[None, :, None]).astype(bf16)
    outgoing = jnp.dot(
        table.reshape(ep_count * share, group_size), normed, preferred_element_type=f32
    ).astype(bf16)
    arrived = lax.all_to_all(
        outgoing.reshape(ep_count, share, -1), ep, split_axis=0, concat_axis=0, tiled=True
    ).reshape(ep_count * share, -1)
    arrived = after(arrived, *relayed, lent)
    across = lax.ppermute(arrived, "core", other_core)
    pieces = (*own, near, lent, *crossed, *relayed)
    keep, give = expert_rows(place, arrived, across, pieces)
    summed = keep + lax.ppermute(give, "core", other_core).astype(f32)
    returned = lax.all_to_all(
        summed.astype(bf16).reshape(ep_count, share, -1), ep, split_axis=0, concat_axis=0, tiled=True
    ).reshape(ep_count * share, -1)

    shifted = jnp.where(hits, after(router_logits, arrived), -jnp.inf)
    shifted = jnp.exp(shifted - jnp.max(shifted, axis=1, keepdims=True))
    gates = of_kind(shifted / jnp.sum(shifted, axis=1, keepdims=True))
    weight = jnp.where(slot[:, :, None] == slot_iota[None, None, :], gates[:, :, None], 0.0)
    weight = weight.reshape(group_size, ep_count * share)
    high = lax.reduce_precision(weight, 8, 7)
    both = jnp.concatenate([high.astype(bf16), (weight - high).astype(bf16)], axis=0)
    mixed = jnp.dot(both, returned, preferred_element_type=f32)
    mixed = mixed[:group_size] + mixed[group_size:]

    result = mixed[:, :width]
    for step in range(1, row_count):
        sent = mixed[:, step * width : (step + 1) * width].astype(bf16)
        result = result + ring_send(sent, step).astype(f32)
    return result.astype(bf16)


def solution(mesh):
    ep_count, tp_count = mesh.devices.shape
    fine = Mesh(
        mesh.devices.reshape(ep_count // 2, 2, tp_count // chip_cores, chip_cores),
        ("line", "pair", "x", "core"),
    )
    ep, tp = ("line", "pair"), ("x", "core")
    return jax.shard_map(
        on_device,
        mesh=fine,
        in_specs=(
            P(ep, tp),
            P(tp),
            P(ep, None),
            P(ep, None),
            P(ep, None, tp),
            P(ep, None, tp),
            P(ep, tp, None),
        ),
        out_specs=P(ep, tp),
        check_vma=False,
    )
```

```python
import functools
import jax
import jax.numpy as jnp
from jax import lax
from jax.experimental import pallas as pl
from jax.experimental.pallas import tpu as pltpu
from jax.sharding import Mesh, PartitionSpec as P

epsilon = 1e-05
chip_cores = 2
block = 256
other_core = [(0, 1), (1, 0)]
detoured = 2


def row_pairs(partner, lent=False):
    pairs = []
    for parity in range(2):
        turn = 1 - parity if lent else parity
        for part in range(4):
            source, target = (part + turn) % 4, (partner(part) + turn) % 4
            pairs.append((4 * parity + source, 4 * parity + target))
    return pairs


near_chip = row_pairs(lambda part: part ^ 1)
near_lent = row_pairs(lambda part: part ^ 1, True)
cross_chip = row_pairs(lambda part: 3 - part)
other_row = [(at, (at + 4) % 8) for at in range(8)]


def pick_kernel(kind_ref, gate, up, down, *refs):
    pieces, sems = refs[:-1], refs[-1]
    unit = gate.shape[2]
    copies = []
    first = 0
    for turn, packed in enumerate(pieces):
        first = 0 if turn in (0, 2) else first
        at = 1 - kind_ref[0] if turn < 2 else kind_ref[0]
        for j in range(packed.shape[0]):
            wide = pl.ds((first + j) * block, block)
            for source, target in (
                (gate.at[at, wide, :], packed.at[j, pl.ds(0, block), pl.ds(0, unit)]),
                (up.at[at, wide, :], packed.at[j, pl.ds(0, block), pl.ds(unit, unit)]),
                (down.at[at, :, wide], packed.at[j, pl.ds(block, unit), :]),
            ):
                copies.append(pltpu.make_async_copy(source, target, sems.at[len(copies)]))
        first += packed.shape[0]
    for copy in copies:
        copy.start()
    for copy in copies:
        copy.wait()


def pick_shards(kind, gate, up, down):
    depth, unit = gate.shape[1:]
    count = depth // block
    anywhere = pl.BlockSpec(memory_space=pl.ANY)
    whole = pl.BlockSpec(memory_space=pltpu.VMEM)
    other = [count - detoured, detoured]
    own = [count - detoured, detoured]
    picked = pl.pallas_call(
        pick_kernel,
        out_shape=tuple(
            jax.ShapeDtypeStruct((size, block + unit, block), gate.dtype) for size in other + own
        ),
        in_specs=[pl.BlockSpec(memory_space=pltpu.SMEM)] + [anywhere] * 3,
        out_specs=(whole,) * 4,
        scratch_shapes=[pltpu.SemaphoreType.DMA((6 * count,))],
        cost_estimate=pl.CostEstimate(flops=0, bytes_accessed=6 * 2**20, transcendentals=0),
    )(kind.reshape(1).astype(jnp.int32), gate, up, down)
    return picked[:2], picked[2:]


def ffn_kernel(count, place_ref, arrived, across, *refs):
    lying, added, (keep, give, hidden, held_shards, sems) = refs[:count], refs[count:-5], refs[-5:]
    total_blocks = held_shards.shape[1]
    copies, first = [], 0
    for n, piece in enumerate(lying):
        into = held_shards.at[first // total_blocks, pl.ds(first % total_blocks, piece.shape[0])]
        copies.append((first // total_blocks, pltpu.make_async_copy(piece, into, sems.at[n])))
        first += piece.shape[0]
    for _, copy in copies:
        copy.start()
    shards = [held_shards.at[k] for k in range(held_shards.shape[0])]
    row, core = place_ref[0], place_ref[1]
    f32 = jnp.float32
    rows, held = arrived.shape
    ring = held // block
    unit = block // 2

    def source(j, parity):
        return 2 * lax.rem(row - j + ring, ring) + parity

    def target(j, parity):
        return 2 * lax.rem(row + j, ring) + parity

    for k, shard in enumerate(shards):
        for shard_of, copy in copies:
            if shard_of == k:
                copy.wait()
        both = jnp.zeros((rows, block), f32)
        for j in range(ring):
            lanes = pl.ds(j * block, block)
            for part, parity in ((arrived, core), (across, 1 - core)):
                both += jnp.dot(
                    part[:, lanes], shard[source(j, parity), :block, :], preferred_element_type=f32
                )
        gate_val, up_val = both[:, :unit], both[:, unit:]
        silu = gate_val / (1.0 + jnp.exp(-gate_val))
        hidden[:, pl.ds(k * unit, unit)] = (silu * up_val).astype(hidden.dtype)
    for which, (parity, out) in enumerate(((core, keep), (1 - core, give))):
        for j in range(ring):
            lanes = pl.ds(j * block, block)
            total = added[which][:, lanes] if added else jnp.zeros((rows, block), f32)
            down = jnp.concatenate([shard[target(j, parity), block:, :] for shard in shards], axis=0)
            total += jnp.dot(hidden[...], down, preferred_element_type=f32)
            out[:, lanes] = total.astype(out.dtype)


def expert_rows(place, arrived, across, pieces, added, give_type):
    rows, held = arrived.shape
    unit, width, count = block // 2, 2 * held, len(pieces)
    blocks = width // block
    shards = sum(piece.shape[0] for piece in pieces) // blocks
    whole = pl.BlockSpec(memory_space=pltpu.VMEM)
    return pl.pallas_call(
        functools.partial(ffn_kernel, count),
        out_shape=(
            jax.ShapeDtypeStruct((rows, held), jnp.float32),
            jax.ShapeDtypeStruct((rows, held), give_type),
        ),
        in_specs=[pl.BlockSpec(memory_space=pltpu.SMEM)]
        + [whole] * 2
        + [pl.BlockSpec(memory_space=pl.ANY)] * count
        + [whole] * len(added),
        out_specs=(whole, whole),
        scratch_shapes=[
            pltpu.VMEM((rows, shards * unit), jnp.bfloat16),
            pltpu.VMEM((shards, blocks, *pieces[0].shape[1:]), jnp.bfloat16),
            pltpu.SemaphoreType.DMA((count,)),
        ],
        compiler_params=pltpu.CompilerParams(vmem_limit_bytes=40 * 2**20),
        cost_estimate=pl.CostEstimate(
            flops=2 * rows * width * unit, bytes_accessed=2**20, transcendentals=0
        ),
    )(place, arrived, across, *pieces, *added)


def on_device(tokens, norm_gain, router_logits, routes, gate_proj, up_proj, down_proj):
    bf16, f32 = jnp.bfloat16, jnp.float32
    ep = ("line", "pair")
    ep_count = lax.axis_size(ep)
    row_count = lax.axis_size("x")
    group_size, width = tokens.shape
    local_experts = gate_proj.shape[0]
    top_count = routes.shape[1]
    expert_count = local_experts * ep_count
    capacity = 2 * group_size * top_count // expert_count
    share = capacity // (row_count // local_experts)
    core = lax.axis_index("core")
    row = lax.axis_index("x")
    split = row_count // local_experts
    part = (row - lax.axis_index("pair")) % row_count
    peers = (row - jnp.arange(ep_count, dtype=jnp.int32) % 2) % row_count

    place = jnp.stack([row, core]).astype(jnp.int32)

    def ring_send(one, step):
        pairs = [(at, (at + step) % row_count) for at in range(row_count)]
        return lax.ppermute(one, "x", pairs)

    padded = lax.pad(tokens, jnp.zeros((), bf16), [(0, 16, 0), (0, 0, 0)])
    at_row = lax.broadcasted_iota(jnp.int32, padded.shape, 0)
    stacked = jnp.where(at_row < group_size, padded, norm_gain[None, :])
    parts = [stacked] + [ring_send(stacked, step) for step in range(1, row_count)]

    other, own = pick_shards(part // split, gate_proj, up_proj, down_proj)
    parts, own, other = lax.optimization_barrier((parts, own, other))

    def send(one, pairs):
        return lax.ppermute(one, ("pair", "x"), pairs)

    def after(one, *others):
        return lax.optimization_barrier((one, *others))[0]

    crossed = [send(other[0], cross_chip)]
    near = send(own[0], near_chip)
    passed = after(send(own[1], other_row), crossed[0], near)
    passed = send(passed, near_lent)
    crossed.append(send(after(other[1], passed), cross_chip))
    lent = send(passed, other_row)
    relayed = [send(after(crossed[0], near), near_chip), send(crossed[1], near_chip)]

    routes = after(routes, own[0])

    expert_iota = jnp.arange(expert_count, dtype=jnp.int32)
    hits = jnp.any(routes[:, :, None] == expert_iota[None, None, :], axis=1)
    earlier = jnp.tril(jnp.ones((group_size, group_size), bf16), -1)
    position = jnp.dot(earlier, hits.astype(bf16), preferred_element_type=f32)

    def of_kind(table):
        table = table.reshape(group_size, ep_count, local_experts)
        return jnp.where((peers // split == 0)[None, :], table[:, :, 0], table[:, :, 1])

    slot = jnp.where(of_kind(hits), of_kind(position), -1.0)
    slot = slot - (peers % split * share).astype(f32)[None, :]
    slot_iota = jnp.arange(share, dtype=jnp.int32).astype(f32)

    floated = [part[:group_size].astype(f32) for part in parts]
    squares = sum(jnp.sum(one * one, axis=1) for one in floated)[None, :]
    squares = squares + lax.ppermute(squares, "core", other_core)
    scale = lax.rsqrt(squares[0] / (width * row_count * chip_cores) + epsilon)[:, None]
    normed = jnp.concatenate(
        [
            (one * scale * part[group_size : group_size + 1].astype(f32)).astype(bf16)
            for one, part in zip(floated, parts)
        ],
        axis=1,
    )

    table = (slot.T[:, None, :] == slot_iota[None, :, None]).astype(bf16)
    outgoing = jnp.dot(
        table.reshape(ep_count * share, group_size), normed, preferred_element_type=f32
    ).astype(bf16)
    arrived = lax.all_to_all(
        outgoing.reshape(ep_count, share, -1), ep, split_axis=0, concat_axis=0, tiled=True
    ).reshape(ep_count * share, -1)
    arrived = after(arrived, relayed[0], lent, crossed[1])
    across = lax.ppermute(arrived, "core", other_core)
    added = expert_rows(place, arrived, across, (*own, near, lent, *crossed), (), f32)
    keep, give = expert_rows(place, arrived, across, relayed, added, bf16)
    summed = keep + lax.ppermute(give, "core", other_core).astype(f32)
    returned = lax.all_to_all(
        summed.astype(bf16).reshape(ep_count, share, -1), ep, split_axis=0, concat_axis=0, tiled=True
    ).reshape(ep_count * share, -1)

    shifted = jnp.where(hits, after(router_logits, arrived), -jnp.inf)
    shifted = jnp.exp(shifted - jnp.max(shifted, axis=1, keepdims=True))
    gates = of_kind(shifted / jnp.sum(shifted, axis=1, keepdims=True))
    weight = jnp.where(slot[:, :, None] == slot_iota[None, None, :], gates[:, :, None], 0.0)
    weight = weight.reshape(group_size, ep_count * share)
    high = lax.reduce_precision(weight, 8, 7)
    both = jnp.concatenate([high.astype(bf16), (weight - high).astype(bf16)], axis=0)
    mixed = jnp.dot(both, returned, preferred_element_type=f32)
    mixed = mixed[:group_size] + mixed[group_size:]

    result = mixed[:, :width]
    for step in range(1, row_count):
        sent = mixed[:, step * width : (step + 1) * width].astype(bf16)
        result = result + ring_send(sent, step).astype(f32)
    return result.astype(bf16)


def solution(mesh):
    ep_count, tp_count = mesh.devices.shape
    fine = Mesh(
        mesh.devices.reshape(ep_count // 2, 2, tp_count // chip_cores, chip_cores),
        ("line", "pair", "x", "core"),
    )
    ep, tp = ("line", "pair"), ("x", "core")
    return jax.shard_map(
        on_device,
        mesh=fine,
        in_specs=(
            P(ep, tp),
            P(tp),
            P(ep, None),
            P(ep, None),
            P(ep, None, tp),
            P(ep, None, tp),
            P(ep, tp, None),
        ),
        out_specs=P(ep, tp),
        check_vma=False,
    )
```

```python
import functools
import jax
import jax.numpy as jnp
from jax import lax
from jax.experimental import pallas as pl
from jax.experimental.pallas import tpu as pltpu
from jax.sharding import Mesh, PartitionSpec as P

epsilon = 1e-05
chip_cores = 2
block = 256
other_core = [(0, 1), (1, 0)]
detoured = 2


def row_pairs(partner, lent=False):
    pairs = []
    for parity in range(2):
        turn = 1 - parity if lent else parity
        for part in range(4):
            source, target = (part + turn) % 4, (partner(part) + turn) % 4
            pairs.append((4 * parity + source, 4 * parity + target))
    return pairs


near_chip = row_pairs(lambda part: part ^ 1)
near_lent = row_pairs(lambda part: part ^ 1, True)
cross_chip = row_pairs(lambda part: 3 - part)
other_row = [(at, (at + 4) % 8) for at in range(8)]


def pick_kernel(kind_ref, gate, up, down, *refs):
    pieces, sems = refs[:-1], refs[-1]
    unit = gate.shape[2]
    copies = []
    first = 0
    for turn, packed in enumerate(pieces):
        first = 0 if turn in (0, 2) else first
        at = 1 - kind_ref[0] if turn < 2 else kind_ref[0]
        for j in range(packed.shape[0]):
            wide = pl.ds((first + j) * block, block)
            for source, target in (
                (gate.at[at, wide, :], packed.at[j, pl.ds(0, block), pl.ds(0, unit)]),
                (up.at[at, wide, :], packed.at[j, pl.ds(0, block), pl.ds(unit, unit)]),
                (down.at[at, :, wide], packed.at[j, pl.ds(block, unit), :]),
            ):
                copies.append(pltpu.make_async_copy(source, target, sems.at[len(copies)]))
        first += packed.shape[0]
    for copy in copies:
        copy.start()
    for copy in copies:
        copy.wait()


def pick_shards(kind, gate, up, down):
    depth, unit = gate.shape[1:]
    count = depth // block
    anywhere = pl.BlockSpec(memory_space=pl.ANY)
    whole = pl.BlockSpec(memory_space=pltpu.VMEM)
    other = [count - detoured, detoured]
    own = [count - detoured, detoured]
    picked = pl.pallas_call(
        pick_kernel,
        out_shape=tuple(
            jax.ShapeDtypeStruct((size, block + unit, block), gate.dtype) for size in other + own
        ),
        in_specs=[pl.BlockSpec(memory_space=pltpu.SMEM)] + [anywhere] * 3,
        out_specs=(whole,) * 4,
        scratch_shapes=[pltpu.SemaphoreType.DMA((6 * count,))],
        cost_estimate=pl.CostEstimate(flops=0, bytes_accessed=6 * 2**20, transcendentals=0),
    )(kind.reshape(1).astype(jnp.int32), gate, up, down)
    return picked[:2], picked[2:]


def ffn_kernel(count, last, place_ref, arrived, across, *refs):
    lying, (early, give, hidden, held_shards, sems) = refs[:count], refs[count:]
    total_blocks = held_shards.shape[1]
    copies, first = [], 0
    for n, piece in enumerate(lying):
        into = held_shards.at[first // total_blocks, pl.ds(first % total_blocks, piece.shape[0])]
        copies.append((first // total_blocks, pltpu.make_async_copy(piece, into, sems.at[n])))
        first += piece.shape[0]
    for _, copy in copies:
        copy.start()
    shards = [held_shards.at[k] for k in range(held_shards.shape[0])]
    row, core = place_ref[0], place_ref[1]
    f32 = jnp.float32
    rows, held = arrived.shape
    ring = held // block
    unit = block // 2

    def source(j, parity):
        return 2 * lax.rem(row - j + ring, ring) + parity

    def target(j, parity):
        return 2 * lax.rem(row + j, ring) + parity

    for k, shard in enumerate(shards):
        for shard_of, copy in copies:
            if shard_of == k:
                copy.wait()
        both = jnp.zeros((rows, block), f32)
        for j in range(ring):
            lanes = pl.ds(j * block, block)
            for part, parity in ((arrived, core), (across, 1 - core)):
                both += jnp.dot(
                    part[:, lanes], shard[source(j, parity), :block, :], preferred_element_type=f32
                )
        gate_val, up_val = both[:, :unit], both[:, unit:]
        silu = gate_val / (1.0 + jnp.exp(-gate_val))
        hidden[:, pl.ds(k * unit, unit)] = (silu * up_val).astype(hidden.dtype)
    for parity, out in ((1 - core, give),) if last else ((core, early), (1 - core, give)):
        for j in range(ring):
            lanes = pl.ds(j * block, block)
            down = jnp.concatenate([shard[target(j, parity), block:, :] for shard in shards], axis=0)
            total = jnp.dot(hidden[...], down, preferred_element_type=f32)
            if last:
                total += early[:, lanes]
            out[:, lanes] = total.astype(out.dtype)


def lie(pieces):
    return [pltpu.with_memory_space_constraint(piece, pltpu.HBM) for piece in pieces]


def sums_kernel(count, place_ref, hidden, *refs):
    lying, (added, keep, downs, sems) = refs[:count], refs[count:]
    copies, first = [], 0
    for n, piece in enumerate(lying):
        source = piece.at[:, pl.ds(block, downs.shape[1]), :]
        into = downs.at[pl.ds(first, piece.shape[0])]
        copies.append(pltpu.make_async_copy(source, into, sems.at[n]))
        first += piece.shape[0]
    for copy in copies:
        copy.start()
    for copy in copies:
        copy.wait()
    row, core = place_ref[0], place_ref[1]
    ring = keep.shape[1] // block
    for j in range(ring):
        lanes = pl.ds(j * block, block)
        down = downs[2 * lax.rem(row + j, ring) + core]
        keep[:, lanes] = added[:, lanes] + jnp.dot(
            hidden[...], down, preferred_element_type=jnp.float32
        )


def kept_sums(place, hidden, pieces, added):
    count = len(pieces)
    blocks = sum(piece.shape[0] for piece in pieces)
    whole = pl.BlockSpec(memory_space=pltpu.VMEM)
    return pl.pallas_call(
        functools.partial(sums_kernel, count),
        out_shape=jax.ShapeDtypeStruct(added.shape, added.dtype),
        in_specs=[pl.BlockSpec(memory_space=pltpu.SMEM), whole]
        + [pl.BlockSpec(memory_space=pl.ANY)] * count
        + [whole],
        out_specs=whole,
        scratch_shapes=[
            pltpu.VMEM((blocks, block // 2, block), jnp.bfloat16),
            pltpu.SemaphoreType.DMA((count,)),
        ],
        compiler_params=pltpu.CompilerParams(vmem_limit_bytes=40 * 2**20),
        cost_estimate=pl.CostEstimate(
            flops=2 * hidden.size * added.shape[1], bytes_accessed=2**20, transcendentals=0
        ),
    )(place, hidden, *lie(pieces), added)


def expert_rows(place, arrived, across, pieces, early=None):
    rows, held = arrived.shape
    unit, width, count = block // 2, 2 * held, len(pieces)
    blocks = width // block
    shards = sum(piece.shape[0] for piece in pieces) // blocks
    last = early is not None
    sums = jax.ShapeDtypeStruct((rows, held), jnp.float32)
    leaving = jax.ShapeDtypeStruct((rows, held), jnp.bfloat16)
    hidden = jax.ShapeDtypeStruct((rows, shards * unit), jnp.bfloat16)
    whole = pl.BlockSpec(memory_space=pltpu.VMEM)
    return pl.pallas_call(
        functools.partial(ffn_kernel, count, last),
        out_shape=(leaving, hidden) if last else (sums, sums),
        in_specs=[pl.BlockSpec(memory_space=pltpu.SMEM)]
        + [whole] * 2
        + [pl.BlockSpec(memory_space=pl.ANY)] * count
        + [whole] * last,
        out_specs=(whole, whole),
        scratch_shapes=([] if last else [pltpu.VMEM(hidden.shape, hidden.dtype)])
        + [
            pltpu.VMEM((shards, blocks, *pieces[0].shape[1:]), jnp.bfloat16),
            pltpu.SemaphoreType.DMA((count,)),
        ],
        compiler_params=pltpu.CompilerParams(vmem_limit_bytes=40 * 2**20),
        cost_estimate=pl.CostEstimate(
            flops=2 * rows * width * unit, bytes_accessed=2**20, transcendentals=0
        ),
    )(place, arrived, across, *lie(pieces), *([early] if last else []))


def on_device(tokens, norm_gain, router_logits, routes, gate_proj, up_proj, down_proj):
    bf16, f32 = jnp.bfloat16, jnp.float32
    ep = ("line", "pair")
    ep_count = lax.axis_size(ep)
    row_count = lax.axis_size("x")
    group_size, width = tokens.shape
    local_experts = gate_proj.shape[0]
    top_count = routes.shape[1]
    expert_count = local_experts * ep_count
    capacity = 2 * group_size * top_count // expert_count
    share = capacity // (row_count // local_experts)
    core = lax.axis_index("core")
    row = lax.axis_index("x")
    split = row_count // local_experts
    part = (row - lax.axis_index("pair")) % row_count
    peers = (row - jnp.arange(ep_count, dtype=jnp.int32) % 2) % row_count

    place = jnp.stack([row, core]).astype(jnp.int32)

    def ring_send(one, step):
        pairs = [(at, (at + step) % row_count) for at in range(row_count)]
        return lax.ppermute(one, "x", pairs)

    padded = lax.pad(tokens, jnp.zeros((), bf16), [(0, 16, 0), (0, 0, 0)])
    at_row = lax.broadcasted_iota(jnp.int32, padded.shape, 0)
    stacked = jnp.where(at_row < group_size, padded, norm_gain[None, :])
    parts = [stacked] + [ring_send(stacked, step) for step in range(1, row_count)]

    other, own = pick_shards(part // split, gate_proj, up_proj, down_proj)
    parts, own, other = lax.optimization_barrier((parts, own, other))

    def send(one, pairs):
        return lax.ppermute(one, ("pair", "x"), pairs)

    def after(one, *others):
        return lax.optimization_barrier((one, *others))[0]

    crossed = [send(other[0], cross_chip)]
    near = send(own[0], near_chip)
    hopped = send(own[1], other_row)
    passed = send(after(hopped, crossed[0], near), near_lent)
    crossed.append(send(after(other[1], passed), cross_chip))
    lent = send(passed, other_row)
    relayed = [send(after(crossed[0], near), near_chip), send(crossed[1], near_chip)]

    routes = after(routes, own[0])

    expert_iota = jnp.arange(expert_count, dtype=jnp.int32)
    hits = jnp.any(routes[:, :, None] == expert_iota[None, None, :], axis=1)
    earlier = jnp.tril(jnp.ones((group_size, group_size), bf16), -1)
    position = jnp.dot(earlier, hits.astype(bf16), preferred_element_type=f32)

    def of_kind(table):
        table = table.reshape(group_size, ep_count, local_experts)
        return jnp.where((peers // split == 0)[None, :], table[:, :, 0], table[:, :, 1])

    slot = jnp.where(of_kind(hits), of_kind(position), -1.0)
    slot = slot - (peers % split * share).astype(f32)[None, :]
    slot_iota = jnp.arange(share, dtype=jnp.int32).astype(f32)

    floated = [part[:group_size].astype(f32) for part in parts]
    squares = sum(jnp.sum(one * one, axis=1) for one in floated)[None, :]
    squares = squares + lax.ppermute(squares, "core", other_core)
    scale = lax.rsqrt(squares[0] / (width * row_count * chip_cores) + epsilon)[:, None]
    normed = jnp.concatenate(
        [
            (one * scale * part[group_size : group_size + 1].astype(f32)).astype(bf16)
            for one, part in zip(floated, parts)
        ],
        axis=1,
    )

    table = (slot.T[:, None, :] == slot_iota[None, :, None]).astype(bf16)
    outgoing = jnp.dot(
        table.reshape(ep_count * share, group_size), normed, preferred_element_type=f32
    ).astype(bf16)
    outgoing = after(outgoing, hopped)
    arrived = lax.all_to_all(
        outgoing.reshape(ep_count, share, -1), ep, split_axis=0, concat_axis=0, tiled=True
    ).reshape(ep_count * share, -1)
    arrived = after(arrived, relayed[0], lent, crossed[1])
    across = lax.ppermute(arrived, "core", other_core)
    kept, leaving = expert_rows(place, arrived, across, (*own, near, lent, *crossed))
    give, hidden = expert_rows(place, arrived, across, relayed, leaving)
    keep = kept_sums(place, hidden, relayed, kept)
    summed = keep + lax.ppermute(give, "core", other_core).astype(f32)
    returned = lax.all_to_all(
        summed.astype(bf16).reshape(ep_count, share, -1), ep, split_axis=0, concat_axis=0, tiled=True
    ).reshape(ep_count * share, -1)

    shifted = jnp.where(hits, after(router_logits, arrived), -jnp.inf)
    shifted = jnp.exp(shifted - jnp.max(shifted, axis=1, keepdims=True))
    gates = of_kind(shifted / jnp.sum(shifted, axis=1, keepdims=True))
    weight = jnp.where(slot[:, :, None] == slot_iota[None, None, :], gates[:, :, None], 0.0)
    weight = weight.reshape(group_size, ep_count * share)
    high = lax.reduce_precision(weight, 8, 7)
    both = jnp.concatenate([high.astype(bf16), (weight - high).astype(bf16)], axis=0)
    mixed = jnp.dot(both, returned, preferred_element_type=f32)
    mixed = mixed[:group_size] + mixed[group_size:]

    result = mixed[:, :width]
    for step in range(1, row_count):
        sent = mixed[:, step * width : (step + 1) * width].astype(bf16)
        result = result + ring_send(sent, step).astype(f32)
    return result.astype(bf16)


def solution(mesh):
    ep_count, tp_count = mesh.devices.shape
    fine = Mesh(
        mesh.devices.reshape(ep_count // 2, 2, tp_count // chip_cores, chip_cores),
        ("line", "pair", "x", "core"),
    )
    ep, tp = ("line", "pair"), ("x", "core")
    return jax.shard_map(
        on_device,
        mesh=fine,
        in_specs=(
            P(ep, tp),
            P(tp),
            P(ep, None),
            P(ep, None),
            P(ep, None, tp),
            P(ep, None, tp),
            P(ep, tp, None),
        ),
        out_specs=P(ep, tp),
        check_vma=False,
    )
```

```python
import functools
import jax
import jax.numpy as jnp
from jax import lax
from jax.experimental import pallas as pl
from jax.experimental.pallas import tpu as pltpu
from jax.sharding import Mesh, PartitionSpec as P

epsilon = 1e-05
chip_cores = 2
block = 256
other_core = [(0, 1), (1, 0)]
detoured = 2


def row_pairs(partner, lent=False):
    pairs = []
    for parity in range(2):
        turn = 1 - parity if lent else parity
        for part in range(4):
            source, target = (part + turn) % 4, (partner(part) + turn) % 4
            pairs.append((4 * parity + source, 4 * parity + target))
    return pairs


near_chip = row_pairs(lambda part: part ^ 1)
near_lent = row_pairs(lambda part: part ^ 1, True)
cross_chip = row_pairs(lambda part: 3 - part)
other_row = [(at, (at + 4) % 8) for at in range(8)]


def pick_kernel(kind_ref, gate, up, down, *refs):
    pieces, scratch, (sems, out_sems) = refs[:4], refs[4:8], refs[8:]
    unit = gate.shape[3]
    loads, used, first = [], 0, 0
    for turn, packed in enumerate(scratch):
        first = 0 if turn in (0, 2) else first
        at = 1 - kind_ref[0] if turn < 2 else kind_ref[0]
        size = packed.shape[0]
        pairs = [
            (gate.at[at, pl.ds(first, size)], packed.at[:, pl.ds(0, block), pl.ds(0, unit)]),
            (up.at[at, pl.ds(first, size)], packed.at[:, pl.ds(0, block), pl.ds(unit, unit)]),
        ]
        for j in range(size):
            wide = pl.ds((first + j) * block, block)
            pairs.append((down.at[at, :, wide], packed.at[j, pl.ds(block, unit), :]))
        first += size
        loads.append([])
        for source, target in pairs:
            loads[-1].append(pltpu.make_async_copy(source, target, sems.at[used]))
            used += 1
    order = (0, 2, 1, 3)
    for turn in order:
        for copy in loads[turn]:
            copy.start()
    stores = [pltpu.make_async_copy(scratch[n], pieces[n], out_sems.at[n]) for n in range(4)]
    for turn in order:
        for copy in loads[turn]:
            copy.wait()
        stores[turn].start()
    for turn in order:
        stores[turn].wait()


def pick_shards(kind, gate, up, down):
    experts, depth, unit = gate.shape
    count = depth // block
    sizes = (count - detoured, detoured) * 2
    shapes = [(size, block + unit, block) for size in sizes]
    anywhere = pl.BlockSpec(memory_space=pl.ANY)
    picked = pl.pallas_call(
        pick_kernel,
        out_shape=tuple(jax.ShapeDtypeStruct(shape, gate.dtype) for shape in shapes),
        in_specs=[pl.BlockSpec(memory_space=pltpu.SMEM)] + [anywhere] * 3,
        out_specs=(pl.BlockSpec(memory_space=pltpu.HBM),) * 4,
        scratch_shapes=[pltpu.VMEM(shape, gate.dtype) for shape in shapes]
        + [pltpu.SemaphoreType.DMA((8 + 2 * count,)), pltpu.SemaphoreType.DMA((4,))],
        cost_estimate=pl.CostEstimate(flops=0, bytes_accessed=6 * 2**20, transcendentals=0),
    )(
        kind.reshape(1).astype(jnp.int32),
        gate.reshape(experts, count, block, unit),
        up.reshape(experts, count, block, unit),
        down,
    )
    return picked[:2], picked[2:]


def ffn_kernel(count, last, place_ref, arrived, across, *refs):
    lying, (early, give, hidden, held_shards, sems) = refs[:count], refs[count:]
    total_blocks = held_shards.shape[1]
    copies, first = [], 0
    for n, piece in enumerate(lying):
        into = held_shards.at[first // total_blocks, pl.ds(first % total_blocks, piece.shape[0])]
        copies.append((first // total_blocks, pltpu.make_async_copy(piece, into, sems.at[n])))
        first += piece.shape[0]
    for _, copy in copies:
        copy.start()
    shards = [held_shards.at[k] for k in range(held_shards.shape[0])]
    row, core = place_ref[0], place_ref[1]
    f32 = jnp.float32
    rows, held = arrived.shape
    ring = held // block
    unit = block // 2

    def source(j, parity):
        return 2 * lax.rem(row - j + ring, ring) + parity

    def target(j, parity):
        return 2 * lax.rem(row + j, ring) + parity

    for k, shard in enumerate(shards):
        for shard_of, copy in copies:
            if shard_of == k:
                copy.wait()
        both = jnp.zeros((rows, block), f32)
        for j in range(ring):
            lanes = pl.ds(j * block, block)
            for part, parity in ((arrived, core), (across, 1 - core)):
                both += jnp.dot(
                    part[:, lanes], shard[source(j, parity), :block, :], preferred_element_type=f32
                )
        gate_val, up_val = both[:, :unit], both[:, unit:]
        silu = gate_val / (1.0 + jnp.exp(-gate_val))
        hidden[:, pl.ds(k * unit, unit)] = (silu * up_val).astype(hidden.dtype)
    for parity, out in ((1 - core, give),) if last else ((core, early), (1 - core, give)):
        for j in range(ring):
            lanes = pl.ds(j * block, block)
            down = jnp.concatenate([shard[target(j, parity), block:, :] for shard in shards], axis=0)
            total = jnp.dot(hidden[...], down, preferred_element_type=f32)
            if last:
                total += early[:, lanes]
            out[:, lanes] = total.astype(out.dtype)


def lie(pieces):
    return [pltpu.with_memory_space_constraint(piece, pltpu.HBM) for piece in pieces]


def sums_kernel(count, place_ref, hidden, *refs):
    lying, (added, keep, downs, sems) = refs[:count], refs[count:]
    copies, first = [], 0
    for n, piece in enumerate(lying):
        source = piece.at[:, pl.ds(block, downs.shape[1]), :]
        into = downs.at[pl.ds(first, piece.shape[0])]
        copies.append(pltpu.make_async_copy(source, into, sems.at[n]))
        first += piece.shape[0]
    for copy in copies:
        copy.start()
    for copy in copies:
        copy.wait()
    row, core = place_ref[0], place_ref[1]
    ring = keep.shape[1] // block
    for j in range(ring):
        lanes = pl.ds(j * block, block)
        down = downs[2 * lax.rem(row + j, ring) + core]
        keep[:, lanes] = added[:, lanes] + jnp.dot(
            hidden[...], down, preferred_element_type=jnp.float32
        )


def kept_sums(place, hidden, pieces, added):
    count = len(pieces)
    blocks = sum(piece.shape[0] for piece in pieces)
    whole = pl.BlockSpec(memory_space=pltpu.VMEM)
    return pl.pallas_call(
        functools.partial(sums_kernel, count),
        out_shape=jax.ShapeDtypeStruct(added.shape, added.dtype),
        in_specs=[pl.BlockSpec(memory_space=pltpu.SMEM), whole]
        + [pl.BlockSpec(memory_space=pl.ANY)] * count
        + [whole],
        out_specs=whole,
        scratch_shapes=[
            pltpu.VMEM((blocks, block // 2, block), jnp.bfloat16),
            pltpu.SemaphoreType.DMA((count,)),
        ],
        compiler_params=pltpu.CompilerParams(vmem_limit_bytes=40 * 2**20),
        cost_estimate=pl.CostEstimate(
            flops=2 * hidden.size * added.shape[1], bytes_accessed=2**20, transcendentals=0
        ),
    )(place, hidden, *lie(pieces), added)


def expert_rows(place, arrived, across, pieces, early=None):
    rows, held = arrived.shape
    unit, width, count = block // 2, 2 * held, len(pieces)
    blocks = width // block
    shards = sum(piece.shape[0] for piece in pieces) // blocks
    last = early is not None
    sums = jax.ShapeDtypeStruct((rows, held), jnp.float32)
    leaving = jax.ShapeDtypeStruct((rows, held), jnp.bfloat16)
    hidden = jax.ShapeDtypeStruct((rows, shards * unit), jnp.bfloat16)
    whole = pl.BlockSpec(memory_space=pltpu.VMEM)
    return pl.pallas_call(
        functools.partial(ffn_kernel, count, last),
        out_shape=(leaving, hidden) if last else (sums, sums),
        in_specs=[pl.BlockSpec(memory_space=pltpu.SMEM)]
        + [whole] * 2
        + [pl.BlockSpec(memory_space=pl.ANY)] * count
        + [whole] * last,
        out_specs=(whole, whole),
        scratch_shapes=([] if last else [pltpu.VMEM(hidden.shape, hidden.dtype)])
        + [
            pltpu.VMEM((shards, blocks, *pieces[0].shape[1:]), jnp.bfloat16),
            pltpu.SemaphoreType.DMA((count,)),
        ],
        compiler_params=pltpu.CompilerParams(vmem_limit_bytes=40 * 2**20),
        cost_estimate=pl.CostEstimate(
            flops=2 * rows * width * unit, bytes_accessed=2**20, transcendentals=0
        ),
    )(place, arrived, across, *lie(pieces), *([early] if last else []))


def on_device(tokens, norm_gain, router_logits, routes, gate_proj, up_proj, down_proj):
    bf16, f32 = jnp.bfloat16, jnp.float32
    ep = ("line", "pair")
    ep_count = lax.axis_size(ep)
    row_count = lax.axis_size("x")
    group_size, width = tokens.shape
    local_experts = gate_proj.shape[0]
    top_count = routes.shape[1]
    expert_count = local_experts * ep_count
    capacity = 2 * group_size * top_count // expert_count
    share = capacity // (row_count // local_experts)
    core = lax.axis_index("core")
    row = lax.axis_index("x")
    split = row_count // local_experts
    part = (row - lax.axis_index("pair")) % row_count
    peers = (row - jnp.arange(ep_count, dtype=jnp.int32) % 2) % row_count

    place = jnp.stack([row, core]).astype(jnp.int32)

    def ring_send(one, step):
        pairs = [(at, (at + step) % row_count) for at in range(row_count)]
        return lax.ppermute(one, "x", pairs)

    padded = lax.pad(tokens, jnp.zeros((), bf16), [(0, 16, 0), (0, 0, 0)])
    at_row = lax.broadcasted_iota(jnp.int32, padded.shape, 0)
    stacked = jnp.where(at_row < group_size, padded, norm_gain[None, :])
    parts = [stacked] + [ring_send(stacked, step) for step in range(1, row_count)]

    other, own = pick_shards(part // split, gate_proj, up_proj, down_proj)
    parts, own, other = lax.optimization_barrier((parts, own, other))

    def send(one, pairs):
        return lax.ppermute(one, ("pair", "x"), pairs)

    def after(one, *others):
        return lax.optimization_barrier((one, *others))[0]

    crossed = [send(other[0], cross_chip)]
    near = send(own[0], near_chip)
    hopped = send(own[1], other_row)
    passed = send(after(hopped, crossed[0], near), near_lent)
    crossed.append(send(after(other[1], passed), cross_chip))
    lent = send(passed, other_row)
    relayed = [send(after(crossed[0], near), near_chip), send(crossed[1], near_chip)]

    routes = after(routes, own[0])

    expert_iota = jnp.arange(expert_count, dtype=jnp.int32)
    hits = jnp.any(routes[:, :, None] == expert_iota[None, None, :], axis=1)
    earlier = jnp.tril(jnp.ones((group_size, group_size), bf16), -1)
    position = jnp.dot(earlier, hits.astype(bf16), preferred_element_type=f32)

    def of_kind(table):
        table = table.reshape(group_size, ep_count, local_experts)
        return jnp.where((peers // split == 0)[None, :], table[:, :, 0], table[:, :, 1])

    slot = jnp.where(of_kind(hits), of_kind(position), -1.0)
    slot = slot - (peers % split * share).astype(f32)[None, :]
    slot_iota = jnp.arange(share, dtype=jnp.int32).astype(f32)

    floated = [part[:group_size].astype(f32) for part in parts]
    squares = sum(jnp.sum(one * one, axis=1) for one in floated)[None, :]
    squares = squares + lax.ppermute(squares, "core", other_core)
    scale = lax.rsqrt(squares[0] / (width * row_count * chip_cores) + epsilon)[:, None]
    normed = jnp.concatenate(
        [
            (one * scale * part[group_size : group_size + 1].astype(f32)).astype(bf16)
            for one, part in zip(floated, parts)
        ],
        axis=1,
    )

    table = (slot.T[:, None, :] == slot_iota[None, :, None]).astype(bf16)
    outgoing = jnp.dot(
        table.reshape(ep_count * share, group_size), normed, preferred_element_type=f32
    ).astype(bf16)
    outgoing = after(outgoing, hopped)
    arrived = lax.all_to_all(
        outgoing.reshape(ep_count, share, -1), ep, split_axis=0, concat_axis=0, tiled=True
    ).reshape(ep_count * share, -1)
    arrived = after(arrived, relayed[0], lent, crossed[1])
    across = lax.ppermute(arrived, "core", other_core)
    kept, leaving = expert_rows(place, arrived, across, (*own, near, lent, *crossed))
    give, hidden = expert_rows(place, arrived, across, relayed, leaving)
    keep = kept_sums(place, hidden, relayed, kept)
    summed = keep + lax.ppermute(give, "core", other_core).astype(f32)
    returned = lax.all_to_all(
        summed.astype(bf16).reshape(ep_count, share, -1), ep, split_axis=0, concat_axis=0, tiled=True
    ).reshape(ep_count * share, -1)

    shifted = jnp.where(hits, after(router_logits, arrived), -jnp.inf)
    shifted = jnp.exp(shifted - jnp.max(shifted, axis=1, keepdims=True))
    gates = of_kind(shifted / jnp.sum(shifted, axis=1, keepdims=True))
    weight = jnp.where(slot[:, :, None] == slot_iota[None, None, :], gates[:, :, None], 0.0)
    weight = weight.reshape(group_size, ep_count * share)
    high = lax.reduce_precision(weight, 8, 7)
    both = jnp.concatenate([high.astype(bf16), (weight - high).astype(bf16)], axis=0)
    mixed = jnp.dot(both, returned, preferred_element_type=f32)
    mixed = mixed[:group_size] + mixed[group_size:]

    result = mixed[:, :width]
    for step in range(1, row_count):
        sent = mixed[:, step * width : (step + 1) * width].astype(bf16)
        result = result + ring_send(sent, step).astype(f32)
    return result.astype(bf16)


def solution(mesh):
    ep_count, tp_count = mesh.devices.shape
    fine = Mesh(
        mesh.devices.reshape(ep_count // 2, 2, tp_count // chip_cores, chip_cores),
        ("line", "pair", "x", "core"),
    )
    ep, tp = ("line", "pair"), ("x", "core")
    return jax.shard_map(
        on_device,
        mesh=fine,
        in_specs=(
            P(ep, tp),
            P(tp),
            P(ep, None),
            P(ep, None),
            P(ep, None, tp),
            P(ep, None, tp),
            P(ep, tp, None),
        ),
        out_specs=P(ep, tp),
        check_vma=False,
    )
```

```python
import functools
import jax
import jax.numpy as jnp
from jax import lax
from jax.experimental import pallas as pl
from jax.experimental.pallas import tpu as pltpu
from jax.sharding import Mesh, PartitionSpec as P

epsilon = 1e-05
chip_cores = 2
block = 256
other_core = [(0, 1), (1, 0)]
detoured = 2


def row_pairs(partner, lent=False):
    pairs = []
    for parity in range(2):
        turn = 1 - parity if lent else parity
        for part in range(4):
            source, target = (part + turn) % 4, (partner(part) + turn) % 4
            pairs.append((4 * parity + source, 4 * parity + target))
    return pairs


near_chip = row_pairs(lambda part: part ^ 1)
near_lent = row_pairs(lambda part: part ^ 1, True)
cross_chip = row_pairs(lambda part: 3 - part)
other_row = [(at, (at + 4) % 8) for at in range(8)]


def pick_kernel(kind_ref, gate, up, down, *refs):
    pieces, scratch, (sems, out_sems) = refs[:4], refs[4:8], refs[8:]
    unit = gate.shape[3]
    loads, used, first = [], 0, 0
    for turn, packed in enumerate(scratch):
        first = 0 if turn in (0, 2) else first
        at = 1 - kind_ref[0] if turn < 2 else kind_ref[0]
        size = packed.shape[0]
        pairs = [
            (gate.at[at, pl.ds(first, size)], packed.at[:, pl.ds(0, block), pl.ds(0, unit)]),
            (up.at[at, pl.ds(first, size)], packed.at[:, pl.ds(0, block), pl.ds(unit, unit)]),
        ]
        for j in range(size):
            wide = pl.ds((first + j) * block, block)
            pairs.append((down.at[at, :, wide], packed.at[j, pl.ds(block, unit), :]))
        first += size
        loads.append([])
        for source, target in pairs:
            loads[-1].append(pltpu.make_async_copy(source, target, sems.at[used]))
            used += 1
    order = (0, 2, 1, 3)
    for turn in order:
        for copy in loads[turn]:
            copy.start()
    stores = [pltpu.make_async_copy(scratch[n], pieces[n], out_sems.at[n]) for n in range(4)]
    for turn in order:
        for copy in loads[turn]:
            copy.wait()
        stores[turn].start()
    for turn in order:
        stores[turn].wait()


def pick_shards(kind, gate, up, down):
    experts, depth, unit = gate.shape
    count = depth // block
    sizes = (count - detoured, detoured) * 2
    shapes = [(size, block + unit, block) for size in sizes]
    anywhere = pl.BlockSpec(memory_space=pl.ANY)
    picked = pl.pallas_call(
        pick_kernel,
        out_shape=tuple(jax.ShapeDtypeStruct(shape, gate.dtype) for shape in shapes),
        in_specs=[pl.BlockSpec(memory_space=pltpu.SMEM)] + [anywhere] * 3,
        out_specs=(pl.BlockSpec(memory_space=pltpu.HBM),) * 4,
        scratch_shapes=[pltpu.VMEM(shape, gate.dtype) for shape in shapes]
        + [pltpu.SemaphoreType.DMA((8 + 2 * count,)), pltpu.SemaphoreType.DMA((4,))],
        cost_estimate=pl.CostEstimate(flops=0, bytes_accessed=6 * 2**20, transcendentals=0),
    )(
        kind.reshape(1).astype(jnp.int32),
        gate.reshape(experts, count, block, unit),
        up.reshape(experts, count, block, unit),
        down,
    )
    return picked[:2], picked[2:]


def ffn_kernel(count, last, place_ref, arrived, across, *refs):
    lying, (early, give, hidden, held_shards, sems) = refs[:count], refs[count:]
    total_blocks = held_shards.shape[1]
    copies, first = [], 0
    for n, piece in enumerate(lying):
        into = held_shards.at[first // total_blocks, pl.ds(first % total_blocks, piece.shape[0])]
        copies.append((first // total_blocks, pltpu.make_async_copy(piece, into, sems.at[n])))
        first += piece.shape[0]
    for _, copy in copies:
        copy.start()
    shards = [held_shards.at[k] for k in range(held_shards.shape[0])]
    row, core = place_ref[0], place_ref[1]
    f32 = jnp.float32
    rows, held = arrived.shape
    ring = held // block
    unit = block // 2

    def source(j, parity):
        return 2 * lax.rem(row - j + ring, ring) + parity

    def target(j, parity):
        return 2 * lax.rem(row + j, ring) + parity

    for k, shard in enumerate(shards):
        for shard_of, copy in copies:
            if shard_of == k:
                copy.wait()
        both = jnp.zeros((rows, block), f32)
        for j in range(ring):
            lanes = pl.ds(j * block, block)
            for part, parity in ((arrived, core), (across, 1 - core)):
                both += jnp.dot(
                    part[:, lanes], shard[source(j, parity), :block, :], preferred_element_type=f32
                )
        gate_val, up_val = both[:, :unit], both[:, unit:]
        silu = gate_val / (1.0 + jnp.exp(-gate_val))
        hidden[:, pl.ds(k * unit, unit)] = (silu * up_val).astype(hidden.dtype)
    for parity, out in ((1 - core, give),) if last else ((core, early), (1 - core, give)):
        for j in range(ring):
            lanes = pl.ds(j * block, block)
            down = jnp.concatenate([shard[target(j, parity), block:, :] for shard in shards], axis=0)
            total = jnp.dot(hidden[...], down, preferred_element_type=f32)
            if last:
                total += early[:, lanes]
            out[:, lanes] = total.astype(out.dtype)


def lie(pieces):
    return [pltpu.with_memory_space_constraint(piece, pltpu.HBM) for piece in pieces]


def sums_kernel(count, place_ref, hidden, *refs):
    lying, (added, keep, downs, sems) = refs[:count], refs[count:]
    copies, first = [], 0
    for n, piece in enumerate(lying):
        source = piece.at[:, pl.ds(block, downs.shape[1]), :]
        into = downs.at[pl.ds(first, piece.shape[0])]
        copies.append(pltpu.make_async_copy(source, into, sems.at[n]))
        first += piece.shape[0]
    for copy in copies:
        copy.start()
    for copy in copies:
        copy.wait()
    row, core = place_ref[0], place_ref[1]
    ring = keep.shape[1] // block
    for j in range(ring):
        lanes = pl.ds(j * block, block)
        down = downs[2 * lax.rem(row + j, ring) + core]
        keep[:, lanes] = added[:, lanes] + jnp.dot(
            hidden[...], down, preferred_element_type=jnp.float32
        )


def kept_sums(place, hidden, pieces, added):
    count = len(pieces)
    blocks = sum(piece.shape[0] for piece in pieces)
    whole = pl.BlockSpec(memory_space=pltpu.VMEM)
    return pl.pallas_call(
        functools.partial(sums_kernel, count),
        out_shape=jax.ShapeDtypeStruct(added.shape, added.dtype),
        in_specs=[pl.BlockSpec(memory_space=pltpu.SMEM), whole]
        + [pl.BlockSpec(memory_space=pl.ANY)] * count
        + [whole],
        out_specs=whole,
        scratch_shapes=[
            pltpu.VMEM((blocks, block // 2, block), jnp.bfloat16),
            pltpu.SemaphoreType.DMA((count,)),
        ],
        compiler_params=pltpu.CompilerParams(vmem_limit_bytes=40 * 2**20),
        cost_estimate=pl.CostEstimate(
            flops=2 * hidden.size * added.shape[1], bytes_accessed=2**20, transcendentals=0
        ),
    )(place, hidden, *lie(pieces), added)


def expert_rows(place, arrived, across, pieces, early=None):
    rows, held = arrived.shape
    unit, width, count = block // 2, 2 * held, len(pieces)
    blocks = width // block
    shards = sum(piece.shape[0] for piece in pieces) // blocks
    last = early is not None
    sums = jax.ShapeDtypeStruct((rows, held), jnp.float32)
    leaving = jax.ShapeDtypeStruct((rows, held), jnp.bfloat16)
    hidden = jax.ShapeDtypeStruct((rows, shards * unit), jnp.bfloat16)
    whole = pl.BlockSpec(memory_space=pltpu.VMEM)
    return pl.pallas_call(
        functools.partial(ffn_kernel, count, last),
        out_shape=(leaving, hidden) if last else (sums, sums),
        in_specs=[pl.BlockSpec(memory_space=pltpu.SMEM)]
        + [whole] * 2
        + [pl.BlockSpec(memory_space=pl.ANY)] * count
        + [whole] * last,
        out_specs=(whole, whole),
        scratch_shapes=([] if last else [pltpu.VMEM(hidden.shape, hidden.dtype)])
        + [
            pltpu.VMEM((shards, blocks, *pieces[0].shape[1:]), jnp.bfloat16),
            pltpu.SemaphoreType.DMA((count,)),
        ],
        compiler_params=pltpu.CompilerParams(vmem_limit_bytes=40 * 2**20),
        cost_estimate=pl.CostEstimate(
            flops=2 * rows * width * unit, bytes_accessed=2**20, transcendentals=0
        ),
    )(place, arrived, across, *lie(pieces), *([early] if last else []))


def on_device(tokens, norm_gain, router_logits, routes, gate_proj, up_proj, down_proj):
    bf16, f32 = jnp.bfloat16, jnp.float32
    ep = ("line", "pair")
    ep_count = lax.axis_size(ep)
    row_count = lax.axis_size("x")
    group_size, width = tokens.shape
    local_experts = gate_proj.shape[0]
    top_count = routes.shape[1]
    expert_count = local_experts * ep_count
    capacity = 2 * group_size * top_count // expert_count
    share = capacity // (row_count // local_experts)
    core = lax.axis_index("core")
    row = lax.axis_index("x")
    split = row_count // local_experts
    part = (row - lax.axis_index("pair")) % row_count
    peers = (row - jnp.arange(ep_count, dtype=jnp.int32) % 2) % row_count

    place = jnp.stack([row, core]).astype(jnp.int32)

    def ring_send(one, step):
        pairs = [(at, (at + step) % row_count) for at in range(row_count)]
        return lax.ppermute(one, "x", pairs)

    other, own = pick_shards(part // split, gate_proj, up_proj, down_proj)
    tokens, other, own = lax.optimization_barrier((tokens, other, own))

    padded = lax.pad(tokens, jnp.zeros((), bf16), [(0, 16, 0), (0, 0, 0)])
    at_row = lax.broadcasted_iota(jnp.int32, padded.shape, 0)
    stacked = jnp.where(at_row < group_size, padded, norm_gain[None, :])
    parts = [stacked] + [ring_send(stacked, step) for step in range(1, row_count)]

    parts, own, other = lax.optimization_barrier((parts, own, other))

    def send(one, pairs):
        return lax.ppermute(one, ("pair", "x"), pairs)

    def after(one, *others):
        return lax.optimization_barrier((one, *others))[0]

    crossed = [send(other[0], cross_chip)]
    near = send(own[0], near_chip)
    hopped = send(own[1], other_row)
    passed = send(after(hopped, crossed[0], near), near_lent)
    crossed.append(send(after(other[1], passed), cross_chip))
    lent = send(passed, other_row)
    relayed = [send(after(crossed[0], near), near_chip), send(crossed[1], near_chip)]

    routes = after(routes, own[0])

    expert_iota = jnp.arange(expert_count, dtype=jnp.int32)
    hits = jnp.any(routes[:, :, None] == expert_iota[None, None, :], axis=1)
    earlier = jnp.tril(jnp.ones((group_size, group_size), bf16), -1)
    position = jnp.dot(earlier, hits.astype(bf16), preferred_element_type=f32)

    def of_kind(table):
        table = table.reshape(group_size, ep_count, local_experts)
        return jnp.where((peers // split == 0)[None, :], table[:, :, 0], table[:, :, 1])

    slot = jnp.where(of_kind(hits), of_kind(position), -1.0)
    slot = slot - (peers % split * share).astype(f32)[None, :]
    slot_iota = jnp.arange(share, dtype=jnp.int32).astype(f32)

    floated = [part[:group_size].astype(f32) for part in parts]
    squares = sum(jnp.sum(one * one, axis=1) for one in floated)[None, :]
    squares = squares + lax.ppermute(squares, "core", other_core)
    scale = lax.rsqrt(squares[0] / (width * row_count * chip_cores) + epsilon)[:, None]
    normed = jnp.concatenate(
        [
            (one * scale * part[group_size : group_size + 1].astype(f32)).astype(bf16)
            for one, part in zip(floated, parts)
        ],
        axis=1,
    )

    table = (slot.T[:, None, :] == slot_iota[None, :, None]).astype(bf16)
    outgoing = jnp.dot(
        table.reshape(ep_count * share, group_size), normed, preferred_element_type=f32
    ).astype(bf16)
    outgoing = after(outgoing, hopped)
    arrived = lax.all_to_all(
        outgoing.reshape(ep_count, share, -1), ep, split_axis=0, concat_axis=0, tiled=True
    ).reshape(ep_count * share, -1)
    arrived = after(arrived, relayed[0], lent, crossed[1])
    across = lax.ppermute(arrived, "core", other_core)
    kept, leaving = expert_rows(place, arrived, across, (*own, near, lent, *crossed))
    give, hidden = expert_rows(place, arrived, across, relayed, leaving)
    keep = kept_sums(place, hidden, relayed, kept)
    summed = keep + lax.ppermute(give, "core", other_core).astype(f32)
    returned = lax.all_to_all(
        summed.astype(bf16).reshape(ep_count, share, -1), ep, split_axis=0, concat_axis=0, tiled=True
    ).reshape(ep_count * share, -1)

    shifted = jnp.where(hits, after(router_logits, arrived), -jnp.inf)
    shifted = jnp.exp(shifted - jnp.max(shifted, axis=1, keepdims=True))
    gates = of_kind(shifted / jnp.sum(shifted, axis=1, keepdims=True))
    weight = jnp.where(slot[:, :, None] == slot_iota[None, None, :], gates[:, :, None], 0.0)
    weight = weight.reshape(group_size, ep_count * share)
    high = lax.reduce_precision(weight, 8, 7)
    both = jnp.concatenate([high.astype(bf16), (weight - high).astype(bf16)], axis=0)
    mixed = jnp.dot(both, returned, preferred_element_type=f32)
    mixed = mixed[:group_size] + mixed[group_size:]

    result = mixed[:, :width]
    for step in range(1, row_count):
        sent = mixed[:, step * width : (step + 1) * width].astype(bf16)
        result = result + ring_send(sent, step).astype(f32)
    return result.astype(bf16)


def solution(mesh):
    ep_count, tp_count = mesh.devices.shape
    fine = Mesh(
        mesh.devices.reshape(ep_count // 2, 2, tp_count // chip_cores, chip_cores),
        ("line", "pair", "x", "core"),
    )
    ep, tp = ("line", "pair"), ("x", "core")
    return jax.shard_map(
        on_device,
        mesh=fine,
        in_specs=(
            P(ep, tp),
            P(tp),
            P(ep, None),
            P(ep, None),
            P(ep, None, tp),
            P(ep, None, tp),
            P(ep, tp, None),
        ),
        out_specs=P(ep, tp),
        check_vma=False,
    )
```

```python
import functools
import jax
import jax.numpy as jnp
from jax import lax
from jax.experimental import pallas as pl
from jax.experimental.pallas import tpu as pltpu
from jax.sharding import Mesh, PartitionSpec as P

epsilon = 1e-05
chip_cores = 2
block = 256
other_core = [(0, 1), (1, 0)]
detoured = 2


def row_pairs(partner, lent=False):
    pairs = []
    for parity in range(2):
        turn = 1 - parity if lent else parity
        for part in range(4):
            source, target = (part + turn) % 4, (partner(part) + turn) % 4
            pairs.append((4 * parity + source, 4 * parity + target))
    return pairs


near_chip = row_pairs(lambda part: part ^ 1)
near_lent = row_pairs(lambda part: part ^ 1, True)
cross_chip = row_pairs(lambda part: 3 - part)
other_row = [(at, (at + 4) % 8) for at in range(8)]


def pick_kernel(kind_ref, gate, up, down, *refs):
    pieces, scratch, (sems, out_sems) = refs[:4], refs[4:8], refs[8:]
    unit = gate.shape[3]
    loads, used, first = [], 0, 0
    for turn, packed in enumerate(scratch):
        first = 0 if turn in (0, 2) else first
        at = 1 - kind_ref[0] if turn < 2 else kind_ref[0]
        size = packed.shape[0]
        pairs = [
            (gate.at[at, pl.ds(first, size)], packed.at[:, pl.ds(0, block), pl.ds(0, unit)]),
            (up.at[at, pl.ds(first, size)], packed.at[:, pl.ds(0, block), pl.ds(unit, unit)]),
        ]
        for j in range(size):
            wide = pl.ds((first + j) * block, block)
            pairs.append((down.at[at, :, wide], packed.at[j, pl.ds(block, unit), :]))
        first += size
        loads.append([])
        for source, target in pairs:
            loads[-1].append(pltpu.make_async_copy(source, target, sems.at[used]))
            used += 1
    order = (0, 2, 1, 3)
    for turn in order:
        for copy in loads[turn]:
            copy.start()
    stores = [pltpu.make_async_copy(scratch[n], pieces[n], out_sems.at[n]) for n in range(4)]
    for turn in order:
        for copy in loads[turn]:
            copy.wait()
        stores[turn].start()
    for turn in order:
        stores[turn].wait()


def pick_shards(kind, gate, up, down):
    experts, depth, unit = gate.shape
    count = depth // block
    sizes = (count - detoured, detoured) * 2
    shapes = [(size, block + unit, block) for size in sizes]
    anywhere = pl.BlockSpec(memory_space=pl.ANY)
    picked = pl.pallas_call(
        pick_kernel,
        out_shape=tuple(jax.ShapeDtypeStruct(shape, gate.dtype) for shape in shapes),
        in_specs=[pl.BlockSpec(memory_space=pltpu.SMEM)] + [anywhere] * 3,
        out_specs=(pl.BlockSpec(memory_space=pltpu.HBM),) * 4,
        scratch_shapes=[pltpu.VMEM(shape, gate.dtype) for shape in shapes]
        + [pltpu.SemaphoreType.DMA((8 + 2 * count,)), pltpu.SemaphoreType.DMA((4,))],
        cost_estimate=pl.CostEstimate(flops=0, bytes_accessed=6 * 2**20, transcendentals=0),
    )(
        kind.reshape(1).astype(jnp.int32),
        gate.reshape(experts, count, block, unit),
        up.reshape(experts, count, block, unit),
        down,
    )
    return picked[:2], picked[2:]


def ffn_kernel(count, last, place_ref, arrived, across, *refs):
    lying, (early, give, hidden, held_shards, sems) = refs[:count], refs[count:]
    total_blocks = held_shards.shape[1]
    copies, first = [], 0
    for n, piece in enumerate(lying):
        into = held_shards.at[first // total_blocks, pl.ds(first % total_blocks, piece.shape[0])]
        copies.append((first // total_blocks, pltpu.make_async_copy(piece, into, sems.at[n])))
        first += piece.shape[0]
    for _, copy in copies:
        copy.start()
    shards = [held_shards.at[k] for k in range(held_shards.shape[0])]
    row, core = place_ref[0], place_ref[1]
    f32 = jnp.float32
    rows, held = arrived.shape
    ring = held // block
    unit = block // 2

    def source(j, parity):
        return 2 * lax.rem(row - j + ring, ring) + parity

    def target(j, parity):
        return 2 * lax.rem(row + j, ring) + parity

    for k, shard in enumerate(shards):
        for shard_of, copy in copies:
            if shard_of == k:
                copy.wait()
        both = jnp.zeros((rows, block), f32)
        for j in range(ring):
            lanes = pl.ds(j * block, block)
            for part, parity in ((arrived, core), (across, 1 - core)):
                both += jnp.dot(
                    part[:, lanes], shard[source(j, parity), :block, :], preferred_element_type=f32
                )
        gate_val, up_val = both[:, :unit], both[:, unit:]
        silu = gate_val / (1.0 + jnp.exp(-gate_val))
        hidden[:, pl.ds(k * unit, unit)] = (silu * up_val).astype(hidden.dtype)
    for parity, out in ((1 - core, give),) if last else ((core, early), (1 - core, give)):
        for j in range(ring):
            lanes = pl.ds(j * block, block)
            down = jnp.concatenate([shard[target(j, parity), block:, :] for shard in shards], axis=0)
            total = jnp.dot(hidden[...], down, preferred_element_type=f32)
            if last:
                total += early[:, lanes]
            out[:, lanes] = total.astype(out.dtype)


def lie(pieces):
    return [pltpu.with_memory_space_constraint(piece, pltpu.HBM) for piece in pieces]


def sums_kernel(count, place_ref, hidden, *refs):
    lying, (added, keep, downs, sems) = refs[:count], refs[count:]
    copies, first = [], 0
    for n, piece in enumerate(lying):
        source = piece.at[:, pl.ds(block, downs.shape[1]), :]
        into = downs.at[pl.ds(first, piece.shape[0])]
        copies.append(pltpu.make_async_copy(source, into, sems.at[n]))
        first += piece.shape[0]
    for copy in copies:
        copy.start()
    for copy in copies:
        copy.wait()
    row, core = place_ref[0], place_ref[1]
    ring = keep.shape[1] // block
    for j in range(ring):
        lanes = pl.ds(j * block, block)
        down = downs[2 * lax.rem(row + j, ring) + core]
        keep[:, lanes] = added[:, lanes] + jnp.dot(
            hidden[...], down, preferred_element_type=jnp.float32
        )


def kept_sums(place, hidden, pieces, added):
    count = len(pieces)
    blocks = sum(piece.shape[0] for piece in pieces)
    whole = pl.BlockSpec(memory_space=pltpu.VMEM)
    return pl.pallas_call(
        functools.partial(sums_kernel, count),
        out_shape=jax.ShapeDtypeStruct(added.shape, added.dtype),
        in_specs=[pl.BlockSpec(memory_space=pltpu.SMEM), whole]
        + [pl.BlockSpec(memory_space=pl.ANY)] * count
        + [whole],
        out_specs=whole,
        scratch_shapes=[
            pltpu.VMEM((blocks, block // 2, block), jnp.bfloat16),
            pltpu.SemaphoreType.DMA((count,)),
        ],
        compiler_params=pltpu.CompilerParams(vmem_limit_bytes=40 * 2**20),
        cost_estimate=pl.CostEstimate(
            flops=2 * hidden.size * added.shape[1], bytes_accessed=2**20, transcendentals=0
        ),
    )(place, hidden, *lie(pieces), added)


def expert_rows(place, arrived, across, pieces, early=None):
    rows, held = arrived.shape
    unit, width, count = block // 2, 2 * held, len(pieces)
    blocks = width // block
    shards = sum(piece.shape[0] for piece in pieces) // blocks
    last = early is not None
    sums = jax.ShapeDtypeStruct((rows, held), jnp.float32)
    leaving = jax.ShapeDtypeStruct((rows, held), jnp.bfloat16)
    hidden = jax.ShapeDtypeStruct((rows, shards * unit), jnp.bfloat16)
    whole = pl.BlockSpec(memory_space=pltpu.VMEM)
    return pl.pallas_call(
        functools.partial(ffn_kernel, count, last),
        out_shape=(leaving, hidden) if last else (sums, sums),
        in_specs=[pl.BlockSpec(memory_space=pltpu.SMEM)]
        + [whole] * 2
        + [pl.BlockSpec(memory_space=pl.ANY)] * count
        + [whole] * last,
        out_specs=(whole, whole),
        scratch_shapes=([] if last else [pltpu.VMEM(hidden.shape, hidden.dtype)])
        + [
            pltpu.VMEM((shards, blocks, *pieces[0].shape[1:]), jnp.bfloat16),
            pltpu.SemaphoreType.DMA((count,)),
        ],
        compiler_params=pltpu.CompilerParams(vmem_limit_bytes=40 * 2**20),
        cost_estimate=pl.CostEstimate(
            flops=2 * rows * width * unit, bytes_accessed=2**20, transcendentals=0
        ),
    )(place, arrived, across, *(list(pieces[:1]) + lie(pieces[1:]) if last else lie(pieces)), *([early] if last else []))


def on_device(tokens, norm_gain, router_logits, routes, gate_proj, up_proj, down_proj):
    bf16, f32 = jnp.bfloat16, jnp.float32
    ep = ("line", "pair")
    ep_count = lax.axis_size(ep)
    row_count = lax.axis_size("x")
    group_size, width = tokens.shape
    local_experts = gate_proj.shape[0]
    top_count = routes.shape[1]
    expert_count = local_experts * ep_count
    capacity = 2 * group_size * top_count // expert_count
    share = capacity // (row_count // local_experts)
    core = lax.axis_index("core")
    row = lax.axis_index("x")
    split = row_count // local_experts
    part = (row - lax.axis_index("pair")) % row_count
    peers = (row - jnp.arange(ep_count, dtype=jnp.int32) % 2) % row_count

    place = jnp.stack([row, core]).astype(jnp.int32)

    def ring_send(one, step):
        pairs = [(at, (at + step) % row_count) for at in range(row_count)]
        return lax.ppermute(one, "x", pairs)

    padded = lax.pad(tokens, jnp.zeros((), bf16), [(0, 16, 0), (0, 0, 0)])
    at_row = lax.broadcasted_iota(jnp.int32, padded.shape, 0)
    stacked = jnp.where(at_row < group_size, padded, norm_gain[None, :])
    parts = [stacked] + [ring_send(stacked, step) for step in range(1, row_count)]

    other, own = pick_shards(part // split, gate_proj, up_proj, down_proj)
    parts, own, other = lax.optimization_barrier((parts, own, other))

    def send(one, pairs):
        return lax.ppermute(one, ("pair", "x"), pairs)

    def after(one, *others):
        return lax.optimization_barrier((one, *others))[0]

    crossed = [send(other[0], cross_chip)]
    near = send(own[0], near_chip)
    hopped = send(own[1], other_row)
    passed = send(after(hopped, crossed[0], near), near_lent)
    crossed.append(send(after(other[1], passed), cross_chip))
    lent = send(passed, other_row)
    relayed = [send(after(crossed[0], near), near_chip), send(crossed[1], near_chip)]

    routes = after(routes, own[0])

    expert_iota = jnp.arange(expert_count, dtype=jnp.int32)
    hits = jnp.any(routes[:, :, None] == expert_iota[None, None, :], axis=1)
    earlier = jnp.tril(jnp.ones((group_size, group_size), bf16), -1)
    position = jnp.dot(earlier, hits.astype(bf16), preferred_element_type=f32)

    def of_kind(table):
        table = table.reshape(group_size, ep_count, local_experts)
        return jnp.where((peers // split == 0)[None, :], table[:, :, 0], table[:, :, 1])

    slot = jnp.where(of_kind(hits), of_kind(position), -1.0)
    slot = slot - (peers % split * share).astype(f32)[None, :]
    slot_iota = jnp.arange(share, dtype=jnp.int32).astype(f32)

    floated = [part[:group_size].astype(f32) for part in parts]
    squares = sum(jnp.sum(one * one, axis=1) for one in floated)[None, :]
    squares = squares + lax.ppermute(squares, "core", other_core)
    scale = lax.rsqrt(squares[0] / (width * row_count * chip_cores) + epsilon)[:, None]
    normed = jnp.concatenate(
        [
            (one * scale * part[group_size : group_size + 1].astype(f32)).astype(bf16)
            for one, part in zip(floated, parts)
        ],
        axis=1,
    )

    table = (slot.T[:, None, :] == slot_iota[None, :, None]).astype(bf16)
    outgoing = jnp.dot(
        table.reshape(ep_count * share, group_size), normed, preferred_element_type=f32
    ).astype(bf16)
    outgoing = after(outgoing, hopped)
    arrived = lax.all_to_all(
        outgoing.reshape(ep_count, share, -1), ep, split_axis=0, concat_axis=0, tiled=True
    ).reshape(ep_count * share, -1)
    arrived = after(arrived, relayed[0], lent, crossed[1])
    across = lax.ppermute(arrived, "core", other_core)
    kept, leaving = expert_rows(place, arrived, across, (*own, near, lent, *crossed))
    give, hidden = expert_rows(place, arrived, across, relayed, leaving)
    keep = kept_sums(place, hidden, relayed, kept)
    summed = keep + lax.ppermute(give, "core", other_core).astype(f32)
    returned = lax.all_to_all(
        summed.astype(bf16).reshape(ep_count, share, -1), ep, split_axis=0, concat_axis=0, tiled=True
    ).reshape(ep_count * share, -1)

    shifted = jnp.where(hits, after(router_logits, arrived), -jnp.inf)
    shifted = jnp.exp(shifted - jnp.max(shifted, axis=1, keepdims=True))
    gates = of_kind(shifted / jnp.sum(shifted, axis=1, keepdims=True))
    weight = jnp.where(slot[:, :, None] == slot_iota[None, None, :], gates[:, :, None], 0.0)
    weight = weight.reshape(group_size, ep_count * share)
    high = lax.reduce_precision(weight, 8, 7)
    both = jnp.concatenate([high.astype(bf16), (weight - high).astype(bf16)], axis=0)
    mixed = jnp.dot(both, returned, preferred_element_type=f32)
    mixed = mixed[:group_size] + mixed[group_size:]

    result = mixed[:, :width]
    for step in range(1, row_count):
        sent = mixed[:, step * width : (step + 1) * width].astype(bf16)
        result = result + ring_send(sent, step).astype(f32)
    return result.astype(bf16)


def solution(mesh):
    ep_count, tp_count = mesh.devices.shape
    fine = Mesh(
        mesh.devices.reshape(ep_count // 2, 2, tp_count // chip_cores, chip_cores),
        ("line", "pair", "x", "core"),
    )
    ep, tp = ("line", "pair"), ("x", "core")
    return jax.shard_map(
        on_device,
        mesh=fine,
        in_specs=(
            P(ep, tp),
            P(tp),
            P(ep, None),
            P(ep, None),
            P(ep, None, tp),
            P(ep, None, tp),
            P(ep, tp, None),
        ),
        out_specs=P(ep, tp),
        check_vma=False,
    )
```
